256 devices in a mesh: seq: 64 (over x_hi, y, z), ch: 4 (over x_lo, core).
Axes of the slice: x: 4 (x_hi: 2, x_lo: 2; x = x_hi * 2 + x_lo), y: 4, z: 8, core: 2. Of those that a mesh axis runs over, the one named last changes fastest.
Arguments:
- signal: bfloat16 [16384, 2048], P('seq', 'ch'), may hold values from -6 to 6
- gate_in: bfloat16 [16384, 2048], P('seq', 'ch'), may hold values from -6 to 6
- skip_gain: float32 [2048], P('ch'), may hold values from -1 to 1
- decay: float32 [2048], P('ch'), may hold values from 6.1035156e-05 to 0.0009765625
- pos_weight1: float32 [33, 64], replicated, may hold values from -16 to 16
- pos_bias1: float32 [64], replicated, may hold values from -4 to 4
- pos_weight2: float32 [64, 64], replicated, may hold values from -0.75 to 0.75
- pos_bias2: float32 [64], replicated, may hold values from -4 to 4
- filt_hi: bfloat16 [64, 2048], P(None, 'ch'), may hold values from -0.75 to 0.75
- filt_fix: int32 [64, 2048], P(None, 'ch'), may hold values from -128 to 127
- out_weight: bfloat16 [2048, 4096], P('ch'), may hold values from -0.125 to 0.125
Outputs:
- mixed: bfloat16 [16384, 4096], P('seq', 'ch')
The draws below stay inside these ranges and needn't reach their ends.
All inputs are finite; a program needn't handle non-finite values.
Results may differ from the reference program's by a relative error of at most 0.005.
Values sent between devices are 32-bit elements; how exact they have to be, the bound alone decides.
A program may use at most 128 MiB of HBM per device.

```python
import math
import jax
import jax.numpy as jnp
from jax import lax

D = 4096
DW = 2048
FW = 64
EMB = 33
SEQLEN = 16384


def place_ends(drawn, stream_key, least, top_value):
    place = [jax.random.randint(jax.random.fold_in(stream_key, axis), (), 0, length) for axis, length in enumerate(drawn.shape)]
    longest = drawn.shape.index(max(drawn.shape))
    next_to = place[:longest] + [(place[longest] + 1) % drawn.shape[longest]] + place[longest + 1:]
    return drawn.at[tuple(place)].set(least).at[tuple(next_to)].set(top_value)


def block_scale(stream_key, dims, shards, low, largest):
    level = 1.0
    for position, shards_of in shards:
        draws = jax.random.uniform(jax.random.fold_in(jax.random.fold_in(stream_key, 6), position), (shards_of,), jnp.float32, low / len(shards), largest / len(shards))
        level = level * jnp.repeat(jnp.exp(draws), dims[position] // shards_of).reshape((-1,) + (1,) * (len(dims) - 1 - position))
    return level


def gaussian(key, extent, spread, bound, shards=(), kind=jnp.bfloat16):
    result = spread * jax.random.normal(key, extent, jnp.float32)
    if shards:
        result = result * block_scale(key, extent, shards, -0.22, 0.18)
    return jnp.clip(result, -bound, bound).astype(kind)


def setup_inputs(seed: int = 0) -> dict:
    key_list = jax.random.split(jax.random.key(seed), 12)
    signal = gaussian(key_list[0], (SEQLEN, DW), 1.0, 6.0, ((0, 64), (1, 4)))
    gate_in = gaussian(key_list[1], (SEQLEN, DW), 1.0, 6.0, ((0, 64), (1, 4)))
    skip_gain = jnp.clip(jax.random.uniform(key_list[2], (DW,), jnp.float32, -1.0, 1.0) * block_scale(key_list[2], (DW,), ((0, 4),), -0.4, 0.0), -1.0, 1.0)
    decay = jnp.clip(jnp.exp(math.log(0.0009765625) - 2.7725887 * jax.random.uniform(key_list[3], (DW,), jnp.float32) ** block_scale(key_list[3], (DW,), ((0, 4),), -0.2, 0.2)), 6.103515625e-05, 0.0009765625)
    pos_weight1 = jnp.clip(jax.random.uniform(key_list[4], (EMB, FW), jnp.float32, -16.0, 16.0), -16.0, 16.0)
    pos_bias1 = gaussian(key_list[5], (FW,), 1.0, 4.0, (), jnp.float32)
    pos_weight2 = jnp.clip(jax.random.uniform(key_list[6], (FW, FW), jnp.float32, -0.75, 0.75), -0.75, 0.75)
    pos_bias2 = gaussian(key_list[7], (FW,), 1.0, 4.0, (), jnp.float32)
    filt_hi = gaussian(key_list[8], (FW, DW), FW ** -0.5, 0.75, ((1, 4),))
    filt_fix = place_ends(jax.random.randint(key_list[9], (FW, DW), -128, 128), jax.random.fold_in(key_list[9], 1), -128, 127).astype(jnp.int32)
    out_weight = gaussian(key_list[10], (DW, D), DW ** -0.5, 0.125, ((0, 4),))
    return dict(signal=signal, gate_in=gate_in, skip_gain=skip_gain, decay=decay, pos_weight1=pos_weight1, pos_bias1=pos_bias1, pos_weight2=pos_weight2, pos_bias2=pos_bias2, filt_hi=filt_hi, filt_fix=filt_fix, out_weight=out_weight)


precise = lax.Precision.HIGHEST

def filter_rows(positions, seq_len, pos_weight1, pos_bias1, pos_weight2, pos_bias2, filter_weight, decay):
    pos_float = positions.astype(jnp.float32)
    harmonics = jnp.arange(1, (pos_weight1.shape[0] - 1) // 2 + 1, dtype=jnp.int32)
    phases = (positions[:, None] * harmonics[None, :] % seq_len).astype(jnp.float32) * (2.0 * math.pi / seq_len)
    features = jnp.concatenate([(pos_float / seq_len)[:, None], jnp.cos(phases), jnp.sin(phases)], axis=1)
    hidden_one = jnp.sin(jnp.dot(features, pos_weight1, precision=precise) + pos_bias1)
    hidden_two = jnp.sin(jnp.dot(hidden_one, pos_weight2, precision=precise) + pos_bias2)
    raw_rows = jnp.dot(hidden_two, filter_weight, precision=precise)
    envelope = jnp.exp(-decay[None, :] * pos_float[:, None]) * jnp.sqrt(2.0 * decay + 1.0 / seq_len)[None, :]
    return raw_rows * envelope

def reference(signal, gate_in, skip_gain, decay, pos_weight1, pos_bias1, pos_weight2, pos_bias2, filt_hi, filt_fix, out_weight):
    filter_weight = filt_hi.astype(jnp.float32) + filt_fix.astype(jnp.float32) * 2.0 ** (-11)
    positions = jnp.arange(SEQLEN, dtype=jnp.int32)
    filters = filter_rows(positions, SEQLEN, pos_weight1, pos_bias1, pos_weight2, pos_bias2, filter_weight, decay)
    signal_f32 = signal.astype(jnp.float32)
    spectrum = jnp.fft.rfft(signal_f32, n=2 * SEQLEN, axis=0) * jnp.fft.rfft(filters, n=2 * SEQLEN, axis=0)
    convolved = jnp.fft.irfft(spectrum, n=2 * SEQLEN, axis=0)[:SEQLEN]
    gated = (gate_in.astype(jnp.float32) * (convolved + skip_gain[None, :] * signal_f32)).astype(jnp.bfloat16)
    return jnp.dot(gated, out_weight, preferred_element_type=jnp.float32).astype(jnp.bfloat16)
```

```python
import math

import jax
import jax.numpy as jnp
from jax import lax
from jax.experimental import pallas as pl
from jax.experimental.pallas import tpu as pltpu
from jax.sharding import PartitionSpec as P

F32 = jnp.float32
BF16 = jnp.bfloat16
MESH = pl.DeviceIdType.MESH

SEQ_LEN = 16384
DEVS = 64
ROWS = 256
CHANS = 512
OWN = 8
HID = 64
PARTS = 4
QUARTER = SEQ_LEN // PARTS
STEP = 256
TAP = 64
DEPTH = 1024
TOP = SEQ_LEN - TAP
COLS = 1024
INV_TURN = 1.0 / (2.0 * math.pi)
COS_POLY = (6.283185159611168, -41.34165492934356, 81.60099819261757, -76.54965682073457, 39.53581371237487)


def turn_cos(turns):
    near = turns - jnp.round(turns)
    arg = 0.25 - jnp.abs(near)
    square = arg * arg
    c0, c1, c2, c3, c4 = COS_POLY
    return arg * (c0 + square * (c1 + square * (c2 + square * (c3 + square * c4))))


def split_two(value):
    high = value.astype(BF16)
    return high, (value - high.astype(F32)).astype(BF16)


def dot(left, right):
    return jnp.dot(left, right, preferred_element_type=F32)


def dot_nt(left, right):
    return lax.dot_general(left, right, (((1,), (1,)), ((), ())), preferred_element_type=F32)


def tile_lanes(value):
    return jnp.concatenate([value] * PARTS, axis=1)


def iota(shape, axis):
    return lax.broadcasted_iota(jnp.int32, shape, axis)


def filter_weights(own_first, decay_ref, w1_ref, b1_ref, w2_ref, b2_ref, hi_ref, fix_ref,
                   first_ref, second_ref, bias_ref, third_ref, env_ref):
    wide = PARTS * HID
    part = iota((16, wide), 1) >> 6
    freq = (iota((16, wide), 0) + 1).astype(F32)
    turns = freq * (TOP - QUARTER * part).astype(F32) * (1.0 / SEQ_LEN)
    cos_top, sin_top = turn_cos(turns), turn_cos(turns - 0.25)
    w_lin = tile_lanes(w1_ref[0:1, :]) * INV_TURN
    w_cos = tile_lanes(w1_ref[1:17, :]) * INV_TURN
    w_sin = tile_lanes(w1_ref[17:33, :]) * INV_TURN
    main = jnp.concatenate(
        [w_cos * cos_top + w_sin * sin_top, w_cos * sin_top - w_sin * cos_top], axis=0
    )
    main_hi = main.astype(BF16).astype(F32)
    main_lo = main - main_hi
    part_row = iota((1, wide), 1) >> 6
    top_row = (TOP - QUARTER * part_row).astype(F32) * (1.0 / SEQ_LEN)
    slope = -w_lin / PARTS
    const = w_lin * top_row + tile_lanes(b1_ref[...]) * INV_TURN - 0.25
    wrap = jnp.where(part_row == PARTS - 1, w_lin, 0.0)
    extra = jnp.zeros((32, wide), F32)
    row = iota((32, wide), 0)
    place = 0
    for value, pieces, repeat in ((slope, 2, 2), (const, 3, 1), (wrap, 3, 1)):
        rest = value
        for _ in range(pieces):
            piece = rest.astype(BF16).astype(F32)
            rest = rest - piece
            for _ in range(repeat):
                extra = jnp.where(row == place, piece, extra)
                place += 1
    first_ref[...] = jnp.concatenate([main_hi, main_hi, main_lo, extra], axis=0).astype(BF16)

    own_block = iota((wide, wide), 0) >> 6 == iota((wide, wide), 1) >> 6
    w2_rows = jnp.concatenate([w2_ref[...] * INV_TURN] * PARTS, axis=0)
    w2_full = jnp.where(own_block, tile_lanes(w2_rows), 0.0)
    w2_hi, w2_lo = split_two(w2_full)
    second_ref[0] = w2_hi
    second_ref[1] = w2_lo
    bias_ref[...] = tile_lanes(b2_ref[...]) * INV_TURN - 0.25

    lhs_rows = PARTS * OWN
    pick = iota((lhs_rows, CHANS), 1) == own_first + (iota((lhs_rows, CHANS), 0) & (OWN - 1))
    chosen = jnp.where(pick, 1.0, 0.0).astype(BF16)
    keep = iota((lhs_rows, wide), 1) >> 6 == iota((lhs_rows, wide), 0) >> 3
    hi_part = jnp.concatenate([hi_ref[...]] * PARTS, axis=0)
    fix_part = jnp.concatenate([(fix_ref[...].astype(F32) * 2.0 ** (-11)).astype(BF16)] * PARTS, axis=0)
    third_ref[...] = jnp.concatenate(
        [jnp.where(keep, dot_nt(chosen, hi_part), 0.0), jnp.where(keep, dot_nt(chosen, fix_part), 0.0)], axis=0
    ).astype(BF16)
    env_ref[...] = jnp.broadcast_to(
        jnp.sum(jnp.where(pick, decay_ref[...], 0.0), axis=1, keepdims=True), (lhs_rows, 128)
    )


def filter_step(step, first_ref, second_ref, bias_ref, third_ref, env_ref, filt_ref):
    lane = iota((STEP, 128), 1)
    where_in = (iota((STEP, 128), 0) + step * STEP).astype(F32)
    freq = ((lane & 15) + 1).astype(F32)
    shift = jnp.where((lane & 16) == 0, 0.0, 0.25)
    value = turn_cos(where_in * freq * (1.0 / SEQ_LEN) - shift)
    value = jnp.where(lane < 96, value, where_in * (1.0 / QUARTER))
    value = jnp.where(lane < 100, value, 1.0)
    value = jnp.where(lane < 103, value, jnp.where(where_in > TOP - QUARTER * (PARTS - 1), 1.0, 0.0))
    value = jnp.where(lane < 106, value, 0.0)
    low = ((lane >= 32) & (lane < 64)) | (lane == 97) | (lane == 99)
    high = value.astype(BF16).astype(F32)
    feats = jnp.where(low, value - high, high).astype(BF16)
    one_hi, one_lo = split_two(turn_cos(dot(feats, first_ref[...])))
    turns = dot(one_hi, second_ref[0]) + dot(one_lo, second_ref[0]) + dot(one_hi, second_ref[1])
    two_hi, two_lo = split_two(turn_cos(turns + bias_ref[...]))
    both = dot_nt(third_ref[...], two_hi) + dot_nt(third_ref[...], two_lo)
    lhs_rows = PARTS * OWN
    shape = (lhs_rows, STEP)
    time = TOP - QUARTER * ((iota(shape, 0) >> 3)) - (iota(shape, 1) + step * STEP)
    time = jnp.where(time < 0, time + SEQ_LEN, time).astype(F32)
    rate = jnp.concatenate([env_ref[...]] * (STEP // 128), axis=1)
    envelope = jnp.exp(-rate * time) * jnp.sqrt(2.0 * rate + 1.0 / SEQ_LEN)
    filters = (both[:lhs_rows] + both[lhs_rows:]) * envelope
    for tile in range(STEP // 128):
        filt_ref[step * (STEP // 128) + tile] = filters[:, 128 * tile:128 * (tile + 1)]


def toeplitz_tiles(chan, filt_ref, toep_ref):
    shape = (TAP, 128)
    ahead = iota(shape, 1) >= iota(shape, 0)
    inside = iota(shape, 1) <= iota(shape, 0) + TAP

    def slanted(tile):
        row = lax.div(tile, QUARTER // 128) * OWN + chan
        taps = filt_ref[lax.rem(tile, QUARTER // 128), pl.ds(row, 1), :]
        return pltpu.roll(jnp.broadcast_to(taps, shape), 0, 1, stride=1, stride_axis=0)

    def block(index, before):
        for sub in range(DEPTH // 128):
            now = slanted(index * (DEPTH // 128) + sub)
            tile = jnp.where(ahead, now, before)
            if sub == DEPTH // 128 - 1:
                tile = jnp.where(inside | (index < SEQ_LEN // DEPTH - 1), tile, 0.0)
            toep_ref[chan, pl.ds(pl.multiple_of(index * TAP, TAP), TAP), sub * 128:(sub + 1) * 128] = tile.astype(BF16)
            before = now
        return before

    lax.fori_loop(0, SEQ_LEN // DEPTH, block, slanted(jnp.int32(SEQ_LEN // 128 - 1)))


def shifted(value, count):
    if count == 0:
        return value
    lane = iota(value.shape, 1) & 63
    return jnp.where(lane >= count, pltpu.roll(value, count, 1), 0.0)


def signal_columns(chan, recv_ref, cols_ref):
    first_half = iota((64, 128), 1) < 64

    def pair(tile):
        return jnp.concatenate([tile, pltpu.roll(tile, 64, 1)], axis=0).T

    low, high = (pair(recv_ref[half, pl.ds(chan, DEVS, stride=OWN), :]) for half in range(2))
    t01, t10, t23, t32 = low[:64], low[64:], high[:64], high[64:]
    t12 = jnp.where(first_half, t10, t32)
    t30 = jnp.where(first_half, shifted(t32, 1), t10)
    for back in range(DEPTH // 64):
        whole, rem = back // 4, back % 4
        if rem == 0:
            left, right = shifted(t01, whole), shifted(t23, whole)
        elif rem == 1:
            left, right = shifted(t30, whole), shifted(t12, whole)
        elif rem == 2:
            left, right = shifted(t23, whole + 1), shifted(t01, whole)
        else:
            left, right = shifted(t12, whole + 1), shifted(t30, whole)
        rows = slice(64 * (15 - back), 64 * (16 - back))
        cols_ref[rows, 0:128] = left.astype(BF16)
        cols_ref[rows, 128:256] = right.astype(BF16)


def convolve(chan, toep_ref, cols_ref, send_ref):
    left = jnp.zeros((64, 128), F32)
    right = jnp.zeros((64, 128), F32)
    for quad in range(4):
        part = dot(toep_ref[chan, 256 * quad:256 * (quad + 1), :], cols_ref[...])
        for sub in range(4):
            left = shifted(left, 4) + part[64 * sub:64 * (sub + 1), 0:128]
            right = shifted(right, 4) + part[64 * sub:64 * (sub + 1), 128:256]
    for half, value in enumerate((left, right)):
        turned = jnp.concatenate([value, pltpu.roll(value, 64, 1)], axis=0).T
        send_ref[half, pl.ds(chan, DEVS, stride=OWN), :] = turned[:64]


def block_kernel(sig_ref, gate_ref, skip_ref, decay_ref, w1_ref, b1_ref, w2_ref, b2_ref, hi_ref, fix_ref, wout_ref,
                 out_ref,
                 first_ref, second_ref, bias_ref, third_ref, env_ref, filt_ref, toep_ref, cols_ref,
                 sig_t, gate_t, recv_x, send_y, recv_y, gated_ref, wide_ref,
                 core_send, core_recv, far_send, far_recv,
                 wide_sem, x_send_sem, x_recv_sem, y_send_sem, y_recv_sem,
                 core_send_sem, core_recv_sem, far_send_sem, far_recv_sem):
    me = lax.axis_index("seq")
    group = lax.axis_index("ch")
    core = lax.rem(group, 2)
    chip = lax.div(group, 2)
    core_mate = chip * 2 + 1 - core
    far_mate = (1 - chip) * 2 + core

    barrier = pltpu.get_barrier_semaphore()

    @pl.loop(1, DEVS)
    def _(step):
        pl.semaphore_signal(barrier, inc=1, device_id={"seq": lax.rem(me + step, DEVS)}, device_id_type=MESH)

    for mate in (core_mate, far_mate):
        pl.semaphore_signal(barrier, inc=1, device_id={"ch": mate}, device_id_type=MESH)

    blocks = ((1 - chip) * 2 + 1 - core, far_mate, core_mate, group)
    loads = [
        pltpu.make_async_copy(
            wout_ref.at[:, pl.ds(pl.multiple_of(block * COLS, COLS), COLS)], wide_ref.at[slot], wide_sem.at[slot]
        )
        for slot, block in enumerate(blocks)
    ]
    for load in loads:
        load.start()

    for half in range(2):
        part = sig_ref[128 * half:128 * (half + 1), :].astype(F32)
        sig_t[half] = part.T
    own_rows = pl.ds(pl.multiple_of(me * OWN, OWN), OWN)
    recv_x[:, own_rows, :] = sig_t[:, own_rows, :]
    pl.semaphore_wait(barrier, DEVS + 1)

    @pl.loop(1, DEVS)
    def _(step):
        peer = lax.rem(me + step, DEVS)
        pltpu.make_async_remote_copy(
            src_ref=sig_t.at[:, pl.ds(pl.multiple_of(peer * OWN, OWN), OWN), :],
            dst_ref=recv_x.at[:, own_rows, :],
            send_sem=x_send_sem,
            recv_sem=x_recv_sem,
            device_id={"seq": peer},
            device_id_type=MESH,
        ).start()

    for half in range(2):
        gate_t[half] = gate_ref[128 * half:128 * (half + 1), :].astype(F32).T
    skip = jnp.broadcast_to(skip_ref[...], (128, CHANS)).T

    filter_weights(me * OWN, decay_ref, w1_ref, b1_ref, w2_ref, b2_ref, hi_ref, fix_ref,
                   first_ref, second_ref, bias_ref, third_ref, env_ref)

    @pl.loop(0, QUARTER // STEP)
    def _(step):
        filter_step(step, first_ref, second_ref, bias_ref, third_ref, env_ref, filt_ref)

    @pl.loop(0, OWN)
    def _(chan):
        toeplitz_tiles(chan, filt_ref, toep_ref)

    many = pl.ds(0, (DEVS - 1) * OWN)
    pltpu.make_async_copy(recv_x.at[:, many, :], recv_x.at[:, many, :], x_recv_sem).wait()

    @pl.loop(0, OWN)
    def _(chan):
        signal_columns(chan, recv_x, cols_ref)
        convolve(chan, toep_ref, cols_ref, send_y)

    for half in range(2):
        recv_y[half, own_rows, :] = send_y[half, own_rows, :]

        @pl.loop(1, DEVS)
        def _(step):
            peer = lax.rem(me + step, DEVS)
            pltpu.make_async_remote_copy(
                src_ref=send_y.at[half, pl.ds(pl.multiple_of(peer * OWN, OWN), OWN), :],
                dst_ref=recv_y.at[half, own_rows, :],
                send_sem=y_send_sem.at[half],
                recv_sem=y_recv_sem.at[half],
                device_id={"seq": peer},
                device_id_type=MESH,
            ).start()

    def to_core(half, which):
        return pltpu.make_async_remote_copy(
            src_ref=core_send.at[half, which], dst_ref=core_recv.at[half, which],
            send_sem=core_send_sem.at[half, which], recv_sem=core_recv_sem.at[half, which],
            device_id={"ch": core_mate}, device_id_type=MESH,
        )

    def to_far(half):
        return pltpu.make_async_remote_copy(
            src_ref=far_send.at[half], dst_ref=far_recv.at[half],
            send_sem=far_send_sem.at[half], recv_sem=far_recv_sem.at[half],
            device_id={"ch": far_mate}, device_id_type=MESH,
        )

    for load in loads:
        load.wait()
    for half in range(2):
        pltpu.make_async_copy(recv_y.at[half, many, :], recv_y.at[half, many, :], y_recv_sem.at[half]).wait()
        gated = gate_t[half] * (recv_y[half] + skip * sig_t[half])
        gated_ref[...] = gated.T.astype(BF16)
        core_send[half, 0] = dot(gated_ref[...], wide_ref[0])
        to_core(half, 0).start()
        far_send[half] = dot(gated_ref[...], wide_ref[1])
        to_core(half, 0).wait_recv()
        far_send[half] += core_recv[half, 0]
        to_far(half).start()
        core_send[half, 1] = dot(gated_ref[...], wide_ref[2])
        to_core(half, 1).start()
        total = dot(gated_ref[...], wide_ref[3])
        to_core(half, 1).wait_recv()
        core_recv[half, 1] += total
    for half in range(2):
        to_far(half).wait_recv()
        out_ref[128 * half:128 * (half + 1), :] = (core_recv[half, 1] + far_recv[half]).astype(BF16)

    pltpu.make_async_copy(sig_t.at[:, many, :], sig_t.at[:, many, :], x_send_sem).wait()
    for half in range(2):
        pltpu.make_async_copy(send_y.at[half, many, :], send_y.at[half, many, :], y_send_sem.at[half]).wait()
        for which in range(2):
            to_core(half, which).wait_send()
        to_far(half).wait_send()


def shards(signal, gate_in, skip_gain, decay, pos_weight1, pos_bias1, pos_weight2, pos_bias2, filt_hi, filt_fix,
           out_weight):
    vmem = pl.BlockSpec(memory_space=pltpu.VMEM)
    wide = PARTS * HID
    return pl.pallas_call(
        block_kernel,
        out_shape=jax.ShapeDtypeStruct((ROWS, COLS), BF16),
        in_specs=[vmem] * 10 + [pl.BlockSpec(memory_space=pl.ANY)],
        out_specs=vmem,
        scratch_shapes=[
            pltpu.VMEM((128, wide), BF16),
            pltpu.VMEM((2, wide, wide), BF16),
            pltpu.VMEM((1, wide), F32),
            pltpu.VMEM((2 * PARTS * OWN, wide), BF16),
            pltpu.VMEM((PARTS * OWN, 128), F32),
            pltpu.VMEM((QUARTER // 128, PARTS * OWN, 128), F32),
            pltpu.VMEM((OWN, SEQ_LEN // DEPTH * TAP, DEPTH), BF16),
            pltpu.VMEM((DEPTH, 256), BF16),
            pltpu.VMEM((2, CHANS, 128), F32),
            pltpu.VMEM((2, CHANS, 128), F32),
            pltpu.VMEM((2, CHANS, 128), F32),
            pltpu.VMEM((2, CHANS, 128), F32),
            pltpu.VMEM((2, CHANS, 128), F32),
            pltpu.VMEM((128, CHANS), BF16),
            pltpu.VMEM((4, CHANS, COLS), BF16),
            pltpu.VMEM((2, 2, 128, COLS), F32),
            pltpu.VMEM((2, 2, 128, COLS), F32),
            pltpu.VMEM((2, 128, COLS), F32),
            pltpu.VMEM((2, 128, COLS), F32),
            pltpu.SemaphoreType.DMA((4,)),
            pltpu.SemaphoreType.DMA,
            pltpu.SemaphoreType.DMA,
            pltpu.SemaphoreType.DMA((2,)),
            pltpu.SemaphoreType.DMA((2,)),
            pltpu.SemaphoreType.DMA((2, 2)),
            pltpu.SemaphoreType.DMA((2, 2)),
            pltpu.SemaphoreType.DMA((2,)),
            pltpu.SemaphoreType.DMA((2,)),
        ],
        compiler_params=pltpu.CompilerParams(
            collective_id=0, has_side_effects=True, vmem_limit_bytes=56 * 2**20
        ),
        name="hyena_block",
    )(
        signal, gate_in, skip_gain[None, :], decay[None, :], pos_weight1, pos_bias1[None, :], pos_weight2,
        pos_bias2[None, :], filt_hi, filt_fix, out_weight,
    )


def solution(mesh):
    return jax.shard_map(
        shards,
        mesh=mesh,
        in_specs=(
            P("seq", "ch"), P("seq", "ch"), P("ch"), P("ch"), P(), P(), P(), P(), P(None, "ch"), P(None, "ch"),
            P("ch", None),
        ),
        out_specs=P("seq", "ch"),
        check_vma=False,
    )
```

```python
import math

import jax
import jax.numpy as jnp
from jax import lax
from jax.experimental import pallas as pl
from jax.experimental.pallas import tpu as pltpu
from jax.sharding import PartitionSpec as P

F32 = jnp.float32
BF16 = jnp.bfloat16
MESH = pl.DeviceIdType.MESH

SEQ_LEN = 16384
DEVS = 64
ROWS = 256
CHANS = 512
OWN = 8
HID = 64
PARTS = 4
QUARTER = SEQ_LEN // PARTS
STEP = 1024
TAP = 16
DEPTH = 1024
DEPTH_PER_PART = QUARTER // DEPTH
TOP = SEQ_LEN - TAP
COLS = 1024
INV_TURN = 1.0 / (2.0 * math.pi)
COS_POLY = (6.283185159611168, -41.34165492934356, 81.60099819261757, -76.54965682073457, 39.53581371237487)


def turn_cos(turns):
    near = turns - jnp.round(turns)
    arg = 0.25 - jnp.abs(near)
    square = arg * arg
    c0, c1, c2, c3, c4 = COS_POLY
    return arg * (c0 + square * (c1 + square * (c2 + square * (c3 + square * c4))))


def split_two(value):
    high = value.astype(BF16)
    return high, (value - high.astype(F32)).astype(BF16)


def dot(left, right):
    return jnp.dot(left, right, preferred_element_type=F32)


def dot_nt(left, right):
    return lax.dot_general(left, right, (((1,), (1,)), ((), ())), preferred_element_type=F32)


def tile_lanes(value):
    return jnp.concatenate([value] * PARTS, axis=1)


def iota(shape, axis):
    return lax.broadcasted_iota(jnp.int32, shape, axis)


def filter_weights(own_first, decay_ref, w1_ref, b1_ref, w2_ref, b2_ref, hi_ref, fix_ref,
                   first_ref, second_ref, bias_ref, third_ref, env_ref):
    wide = PARTS * HID
    part = iota((16, wide), 1) >> 6
    freq = (iota((16, wide), 0) + 1).astype(F32)
    turns = freq * (TOP - QUARTER * part).astype(F32) * (1.0 / SEQ_LEN)
    cos_top, sin_top = turn_cos(turns), turn_cos(turns - 0.25)
    w_lin = tile_lanes(w1_ref[0:1, :]) * INV_TURN
    w_cos = tile_lanes(w1_ref[1:17, :]) * INV_TURN
    w_sin = tile_lanes(w1_ref[17:33, :]) * INV_TURN
    main = jnp.concatenate(
        [w_cos * cos_top + w_sin * sin_top, w_cos * sin_top - w_sin * cos_top], axis=0
    )
    main_hi = main.astype(BF16).astype(F32)
    main_lo = main - main_hi
    part_row = iota((1, wide), 1) >> 6
    top_row = (TOP - QUARTER * part_row).astype(F32) * (1.0 / SEQ_LEN)
    slope = -w_lin / PARTS
    const = w_lin * top_row + tile_lanes(b1_ref[...]) * INV_TURN - 0.25
    wrap = jnp.where(part_row == PARTS - 1, w_lin, 0.0)
    extra = jnp.zeros((32, wide), F32)
    row = iota((32, wide), 0)
    place = 0
    for value, pieces, repeat in ((slope, 2, 2), (const, 3, 1), (wrap, 3, 1)):
        rest = value
        for _ in range(pieces):
            piece = rest.astype(BF16).astype(F32)
            rest = rest - piece
            for _ in range(repeat):
                extra = jnp.where(row == place, piece, extra)
                place += 1
    first_ref[...] = jnp.concatenate([main_hi, main_hi, main_lo, extra], axis=0).astype(BF16)

    own_block = iota((wide, wide), 0) >> 6 == iota((wide, wide), 1) >> 6
    w2_rows = jnp.concatenate([w2_ref[...] * INV_TURN] * PARTS, axis=0)
    w2_full = jnp.where(own_block, tile_lanes(w2_rows), 0.0)
    w2_hi, w2_lo = split_two(w2_full)
    second_ref[0] = w2_hi
    second_ref[1] = w2_lo
    bias_ref[...] = tile_lanes(b2_ref[...]) * INV_TURN - 0.25

    lhs_rows = PARTS * OWN
    pick = iota((lhs_rows, CHANS), 1) == own_first + DEVS * (iota((lhs_rows, CHANS), 0) & (OWN - 1))
    chosen = jnp.where(pick, 1.0, 0.0).astype(BF16)
    keep = iota((lhs_rows, wide), 1) >> 6 == iota((lhs_rows, wide), 0) >> 3
    hi_part = jnp.concatenate([hi_ref[...]] * PARTS, axis=0)
    fix_part = jnp.concatenate([(fix_ref[...].astype(F32) * 2.0 ** (-11)).astype(BF16)] * PARTS, axis=0)
    third_ref[...] = jnp.concatenate(
        [jnp.where(keep, dot_nt(chosen, hi_part), 0.0), jnp.where(keep, dot_nt(chosen, fix_part), 0.0)], axis=0
    ).astype(BF16)
    env_ref[...] = jnp.broadcast_to(
        jnp.sum(jnp.where(pick, decay_ref[...], 0.0), axis=1, keepdims=True), (lhs_rows, 128)
    )


def filter_step(step, first_ref, second_ref, bias_ref, third_ref, env_ref, filt_ref):
    lane = iota((STEP, 128), 1)
    where_in = (iota((STEP, 128), 0) + step * STEP).astype(F32)
    freq = ((lane & 15) + 1).astype(F32)
    shift = jnp.where((lane & 16) == 0, 0.0, 0.25)
    value = turn_cos(where_in * freq * (1.0 / SEQ_LEN) - shift)
    value = jnp.where(lane < 96, value, where_in * (1.0 / QUARTER))
    value = jnp.where(lane < 100, value, 1.0)
    value = jnp.where(lane < 103, value, jnp.where(where_in > TOP - QUARTER * (PARTS - 1), 1.0, 0.0))
    value = jnp.where(lane < 106, value, 0.0)
    low = ((lane >= 32) & (lane < 64)) | (lane == 97) | (lane == 99)
    high = value.astype(BF16).astype(F32)
    feats = jnp.where(low, value - high, high).astype(BF16)
    one_hi, one_lo = split_two(turn_cos(dot(feats, first_ref[...])))
    turns = dot(one_hi, second_ref[0]) + dot(one_lo, second_ref[0]) + dot(one_hi, second_ref[1])
    two_hi, two_lo = split_two(turn_cos(turns + bias_ref[...]))
    both = dot_nt(third_ref[...], two_hi) + dot_nt(third_ref[...], two_lo)
    lhs_rows = PARTS * OWN
    shape = (lhs_rows, STEP)
    time = TOP - QUARTER * ((iota(shape, 0) >> 3)) - (iota(shape, 1) + step * STEP)
    time = jnp.where(time < 0, time + SEQ_LEN, time).astype(F32)
    rate = jnp.concatenate([env_ref[...]] * (STEP // 128), axis=1)
    envelope = jnp.exp(-rate * time) * jnp.sqrt(2.0 * rate + 1.0 / SEQ_LEN)
    filters = (both[:lhs_rows] + both[lhs_rows:]) * envelope
    for tile in range(STEP // 128):
        filt_ref[step * (STEP // 128) + tile] = filters[:, 128 * tile:128 * (tile + 1)]


def toeplitz_tiles(filt_ref, toep_ref):
    shape = (TAP, 128)
    ahead = iota(shape, 1) >= iota(shape, 0)
    inside = iota(shape, 1) <= iota(shape, 0) + (128 - TAP)
    per_part = QUARTER // 128

    def slanted(part, tile):
        taps = filt_ref[tile, pl.ds(pl.multiple_of(part * OWN, OWN), OWN), :]
        return tuple(
            pltpu.roll(jnp.broadcast_to(taps[chan:chan + 1], shape), 0, 1, stride=1, stride_axis=0)
            for chan in range(OWN)
        )

    def block(index, before):
        part = lax.div(index, DEPTH_PER_PART)
        first = lax.rem(index, DEPTH_PER_PART) * (DEPTH // 128)
        for sub in range(DEPTH // 128):
            now = slanted(part, first + sub)
            for chan in range(OWN):
                tile = jnp.where(ahead, now[chan], before[chan])
                if sub == DEPTH // 128 - 1:
                    tile = jnp.where(inside | (index < SEQ_LEN // DEPTH - 1), tile, 0.0)
                toep_ref[chan, pl.ds(pl.multiple_of(index * TAP, TAP), TAP), sub * 128:(sub + 1) * 128] = tile.astype(BF16)
            before = now
        return before

    lax.fori_loop(0, SEQ_LEN // DEPTH, block, slanted(PARTS - 1, per_part - 1))


def signal_windows(chan, recv_ref, rows_ref, win_ref):
    lane = iota((128, 128), 1)
    before = recv_ref[pl.ds(chan, 128, stride=OWN), :]
    after = recv_ref[pl.ds(chan + OWN, 128, stride=OWN), :]
    for sub in range(8):
        ahead = TAP * (sub + 1)
        value = after
        if ahead < 128:
            value = pltpu.roll(jnp.where(lane >= ahead, before, after), 128 - ahead, 1)
        rows_ref[pl.ds(56 + sub, 128, stride=8), :] = value
    win_ref[:, 0:128] = rows_ref[0:1072, :].astype(BF16)
    win_ref[:, 128:256] = rows_ref[8:1080, :].astype(BF16)


def convolve(chan, toep_ref, win_ref, conv_ref):
    sums = ([None] * 8, [None] * 8)
    for cols in range(4):
        window = jnp.concatenate(
            [win_ref[16 * deep + 256 * cols:16 * deep + 256 * (cols + 1), :] for deep in range(DEPTH // 256)], axis=1
        )
        part = dot_nt(toep_ref[chan, 64 * cols:256, :], window)
        for lag in range(16 - 4 * cols):
            row = TAP * (15 - lag - 4 * cols)
            for side in range(2):
                tile = 2 * cols + side + lag // 2
                if tile < 8:
                    piece = part[row:row + TAP, 128 * side:128 * (side + 1)]
                    old = sums[lag % 2][tile]
                    sums[lag % 2][tile] = piece if old is None else old + piece
    first_half = iota((TAP, 128), 1) < 64
    earlier = jnp.zeros((TAP, 128), F32)
    for tile in range(8):
        turned = pltpu.roll(sums[1][tile], 64, 1)
        conv_ref[tile, pl.ds(pl.multiple_of(chan * TAP, TAP), TAP), :] = sums[0][tile] + jnp.where(
            first_half, earlier, turned
        )
        earlier = turned


def block_kernel(sig_ref, gate_ref, skip_ref, decay_ref, w1_ref, b1_ref, w2_ref, b2_ref, hi_ref, fix_ref, wout_ref,
                 out_ref,
                 first_ref, second_ref, bias_ref, third_ref, env_ref, filt_ref, toep_ref, rows_ref, win_ref, conv_ref,
                 send_x, recv_x, send_y, recv_y, gated_ref, wide_ref,
                 core_send, core_recv, far_send, far_recv,
                 wide_sem, x_send_sem, x_recv_sem, y_send_sem, y_recv_sem,
                 core_send_sem, core_recv_sem, far_send_sem, far_recv_sem):
    me = lax.axis_index("seq")
    group = lax.axis_index("ch")
    core = lax.rem(group, 2)
    chip = lax.div(group, 2)
    core_mate = chip * 2 + 1 - core
    far_mate = (1 - chip) * 2 + core

    barrier = pltpu.get_barrier_semaphore()

    @pl.loop(1, DEVS)
    def _(step):
        pl.semaphore_signal(barrier, inc=1, device_id={"seq": lax.rem(me + step, DEVS)}, device_id_type=MESH)

    for mate in (core_mate, far_mate):
        pl.semaphore_signal(barrier, inc=1, device_id={"ch": mate}, device_id_type=MESH)

    blocks = ((1 - chip) * 2 + 1 - core, far_mate, core_mate, group)
    loads = [
        pltpu.make_async_copy(
            wout_ref.at[:, pl.ds(pl.multiple_of(block * COLS, COLS), COLS)], wide_ref.at[slot], wide_sem.at[slot]
        )
        for slot, block in enumerate(blocks)
    ]
    for load in loads:
        load.start()

    for half in range(2):
        turned = sig_ref[128 * half:128 * (half + 1), :].astype(F32).T
        for chan in range(OWN):
            send_x[pl.ds(8 * half + chan, DEVS, stride=16), :] = turned[DEVS * chan:DEVS * (chan + 1), :]
    recv_x[0:OWN, :] = jnp.zeros((OWN, 128), F32)
    own_send = pl.ds(pl.multiple_of(me * 16, 16), 16)
    own_recv = pl.ds(pl.multiple_of(me * 16 + 8, 8), 16)
    recv_x[own_recv, :] = send_x[own_send, :]
    pl.semaphore_wait(barrier, DEVS + 1)

    @pl.loop(1, DEVS)
    def _(step):
        peer = lax.rem(me + step, DEVS)
        pltpu.make_async_remote_copy(
            src_ref=send_x.at[pl.ds(pl.multiple_of(peer * 16, 16), 16), :],
            dst_ref=recv_x.at[own_recv, :],
            send_sem=x_send_sem,
            recv_sem=x_recv_sem,
            device_id={"seq": peer},
            device_id_type=MESH,
        ).start()

    filter_weights(me, decay_ref, w1_ref, b1_ref, w2_ref, b2_ref, hi_ref, fix_ref,
                   first_ref, second_ref, bias_ref, third_ref, env_ref)

    @pl.loop(0, QUARTER // STEP)
    def _(step):
        filter_step(step, first_ref, second_ref, bias_ref, third_ref, env_ref, filt_ref)

    toeplitz_tiles(filt_ref, toep_ref)

    rows_ref[0:56, :] = jnp.zeros((56, 128), F32)
    many = pl.ds(0, (DEVS - 1) * 16)
    pltpu.make_async_copy(recv_x.at[many, :], recv_x.at[many, :], x_recv_sem).wait()

    @pl.loop(0, OWN, unroll=2)
    def _(chan):
        signal_windows(chan, recv_x, rows_ref, win_ref)
        convolve(chan, toep_ref, win_ref, conv_ref)

    for tile in range(8):
        turned = conv_ref[tile].T
        for peer in range(8):
            for half in range(2):
                send_y[half, 64 * tile + 8 * peer:64 * tile + 8 * (peer + 1), :] = (
                    turned[16 * peer + 8 * half:16 * peer + 8 * (half + 1), :]
                )
    own_rows = pl.ds(pl.multiple_of(me * 8, 8), 8)
    for half in range(2):
        recv_y[half, own_rows, :] = send_y[half, own_rows, :]

        @pl.loop(1, DEVS)
        def _(step):
            peer = lax.rem(me + step, DEVS)
            pltpu.make_async_remote_copy(
                src_ref=send_y.at[half, pl.ds(pl.multiple_of(peer * 8, 8), 8), :],
                dst_ref=recv_y.at[half, own_rows, :],
                send_sem=y_send_sem.at[half],
                recv_sem=y_recv_sem.at[half],
                device_id={"seq": peer},
                device_id_type=MESH,
            ).start()

    def to_core(half, which):
        return pltpu.make_async_remote_copy(
            src_ref=core_send.at[half, which], dst_ref=core_recv.at[half, which],
            send_sem=core_send_sem.at[half, which], recv_sem=core_recv_sem.at[half, which],
            device_id={"ch": core_mate}, device_id_type=MESH,
        )

    def to_far(half):
        return pltpu.make_async_remote_copy(
            src_ref=far_send.at[half], dst_ref=far_recv.at[half],
            send_sem=far_send_sem.at[half], recv_sem=far_recv_sem.at[half],
            device_id={"ch": far_mate}, device_id_type=MESH,
        )

    for load in loads:
        load.wait()
    half_rows = pl.ds(0, (DEVS - 1) * 8)
    first_half = iota((16, 128), 1) < 64
    for half in range(2):
        pltpu.make_async_copy(recv_y.at[half, half_rows, :], recv_y.at[half, half_rows, :], y_recv_sem.at[half]).wait()
        for pair in range(4):
            both = jnp.concatenate(
                [recv_y[half, pl.ds(2 * pair + side, DEVS, stride=8), :] for side in range(2)], axis=0
            ).T
            swapped = pltpu.roll(both, 64, 1)
            for two in range(OWN // 2):
                low = slice(32 * two, 32 * two + 16)
                high = slice(32 * two + 16, 32 * two + 32)
                lanes = slice(128 * two, 128 * (two + 1))
                for side, value in enumerate((
                    jnp.where(first_half, both[low], swapped[high]), jnp.where(first_half, swapped[low], both[high])
                )):
                    place = 16 * (2 * pair + side)
                    rows = slice(128 * half + place, 128 * half + place + 16)
                    gated_ref[place:place + 16, lanes] = (
                        gate_ref[rows, lanes].astype(F32)
                        * (value + skip_ref[:, lanes] * sig_ref[rows, lanes].astype(F32))
                    ).astype(BF16)
        core_send[half, 0] = dot(gated_ref[...], wide_ref[0])
        to_core(half, 0).start()
        far_send[half] = dot(gated_ref[...], wide_ref[1])
        to_core(half, 0).wait_recv()
        far_send[half] += core_recv[half, 0]
        to_far(half).start()
        core_send[half, 1] = dot(gated_ref[...], wide_ref[2])
        to_core(half, 1).start()
        total = dot(gated_ref[...], wide_ref[3])
        to_core(half, 1).wait_recv()
        core_recv[half, 1] += total
    for half in range(2):
        to_far(half).wait_recv()
        out_ref[128 * half:128 * (half + 1), :] = (core_recv[half, 1] + far_recv[half]).astype(BF16)

    pltpu.make_async_copy(send_x.at[many, :], send_x.at[many, :], x_send_sem).wait()
    for half in range(2):
        pltpu.make_async_copy(send_y.at[half, half_rows, :], send_y.at[half, half_rows, :], y_send_sem.at[half]).wait()
        for which in range(2):
            to_core(half, which).wait_send()
        to_far(half).wait_send()


def shards(signal, gate_in, skip_gain, decay, pos_weight1, pos_bias1, pos_weight2, pos_bias2, filt_hi, filt_fix,
           out_weight):
    vmem = pl.BlockSpec(memory_space=pltpu.VMEM)
    wide = PARTS * HID
    return pl.pallas_call(
        block_kernel,
        out_shape=jax.ShapeDtypeStruct((ROWS, COLS), BF16),
        in_specs=[vmem] * 10 + [pl.BlockSpec(memory_space=pl.ANY)],
        out_specs=vmem,
        scratch_shapes=[
            pltpu.VMEM((128, wide), BF16),
            pltpu.VMEM((2, wide, wide), BF16),
            pltpu.VMEM((1, wide), F32),
            pltpu.VMEM((2 * PARTS * OWN, wide), BF16),
            pltpu.VMEM((PARTS * OWN, 128), F32),
            pltpu.VMEM((QUARTER // 128, PARTS * OWN, 128), F32),
            pltpu.VMEM((OWN, SEQ_LEN // DEPTH * TAP, DEPTH), BF16),
            pltpu.VMEM((1088, 128), F32),
            pltpu.VMEM((1072, 256), BF16),
            pltpu.VMEM((8, 128, 128), F32),
            pltpu.VMEM((DEVS * 16, 128), F32),
            pltpu.VMEM((DEVS * 16 + 8, 128), F32),
            pltpu.VMEM((2, DEVS * 8, 128), F32),
            pltpu.VMEM((2, DEVS * 8, 128), F32),
            pltpu.VMEM((128, CHANS), BF16),
            pltpu.VMEM((4, CHANS, COLS), BF16),
            pltpu.VMEM((2, 2, 128, COLS), F32),
            pltpu.VMEM((2, 2, 128, COLS), F32),
            pltpu.VMEM((2, 128, COLS), F32),
            pltpu.VMEM((2, 128, COLS), F32),
            pltpu.SemaphoreType.DMA((4,)),
            pltpu.SemaphoreType.DMA,
            pltpu.SemaphoreType.DMA,
            pltpu.SemaphoreType.DMA((2,)),
            pltpu.SemaphoreType.DMA((2,)),
            pltpu.SemaphoreType.DMA((2, 2)),
            pltpu.SemaphoreType.DMA((2, 2)),
            pltpu.SemaphoreType.DMA((2,)),
            pltpu.SemaphoreType.DMA((2,)),
        ],
        compiler_params=pltpu.CompilerParams(
            collective_id=0, has_side_effects=True, vmem_limit_bytes=56 * 2**20
        ),
        name="hyena_block",
    )(
        signal, gate_in, skip_gain[None, :], decay[None, :], pos_weight1, pos_bias1[None, :], pos_weight2,
        pos_bias2[None, :], filt_hi, filt_fix, out_weight,
    )


def solution(mesh):
    return jax.shard_map(
        shards,
        mesh=mesh,
        in_specs=(
            P("seq", "ch"), P("seq", "ch"), P("ch"), P("ch"), P(), P(), P(), P(), P(None, "ch"), P(None, "ch"),
            P("ch", None),
        ),
        out_specs=P("seq", "ch"),
        check_vma=False,
    )
```

```python
import math

import jax
import jax.numpy as jnp
from jax import lax
from jax.experimental import pallas as pl
from jax.experimental.pallas import tpu as pltpu
from jax.sharding import PartitionSpec as P

F32 = jnp.float32
BF16 = jnp.bfloat16
MESH = pl.DeviceIdType.MESH

SEQ_LEN = 16384
DEVS = 64
ROWS = 256
CHANS = 512
OWN = 8
HID = 64
PARTS = 4
QUARTER = SEQ_LEN // PARTS
STEP = 1024
TAP = 16
DEPTH = 1024
DEPTH_PER_PART = QUARTER // DEPTH
TOP = SEQ_LEN - TAP
COLS = 1024
INV_TURN = 1.0 / (2.0 * math.pi)
COS_POLY = (6.283185159611168, -41.34165492934356, 81.60099819261757, -76.54965682073457, 39.53581371237487)


def turn_cos(turns):
    near = turns - jnp.round(turns)
    arg = 0.25 - jnp.abs(near)
    square = arg * arg
    c0, c1, c2, c3, c4 = COS_POLY
    return arg * (c0 + square * (c1 + square * (c2 + square * (c3 + square * c4))))


def split_two(value):
    high = value.astype(BF16)
    return high, (value - high.astype(F32)).astype(BF16)


def dot(left, right):
    return jnp.dot(left, right, preferred_element_type=F32)


def dot_nt(left, right):
    return lax.dot_general(left, right, (((1,), (1,)), ((), ())), preferred_element_type=F32)


def tile_lanes(value):
    return jnp.concatenate([value] * PARTS, axis=1)


def iota(shape, axis):
    return lax.broadcasted_iota(jnp.int32, shape, axis)


def filter_weights(own_first, decay_ref, w1_ref, b1_ref, w2_ref, b2_ref, hi_ref, fix_ref,
                   first_ref, second_ref, bias_ref, third_ref, env_ref):
    wide = PARTS * HID
    part = iota((16, wide), 1) >> 6
    freq = (iota((16, wide), 0) + 1).astype(F32)
    turns = freq * (TOP - QUARTER * part).astype(F32) * (1.0 / SEQ_LEN)
    cos_top, sin_top = turn_cos(turns), turn_cos(turns - 0.25)
    w_lin = tile_lanes(w1_ref[0:1, :]) * INV_TURN
    w_cos = tile_lanes(w1_ref[1:17, :]) * INV_TURN
    w_sin = tile_lanes(w1_ref[17:33, :]) * INV_TURN
    main = jnp.concatenate(
        [w_cos * cos_top + w_sin * sin_top, w_cos * sin_top - w_sin * cos_top], axis=0
    )
    main_hi = main.astype(BF16).astype(F32)
    main_lo = main - main_hi
    part_row = iota((1, wide), 1) >> 6
    top_row = (TOP - QUARTER * part_row).astype(F32) * (1.0 / SEQ_LEN)
    slope = -w_lin / PARTS
    const = w_lin * top_row + tile_lanes(b1_ref[...]) * INV_TURN - 0.25
    wrap = jnp.where(part_row == PARTS - 1, w_lin, 0.0)
    extra = jnp.zeros((32, wide), F32)
    row = iota((32, wide), 0)
    place = 0
    for value, pieces, repeat in ((slope, 2, 2), (const, 3, 1), (wrap, 3, 1)):
        rest = value
        for _ in range(pieces):
            piece = rest.astype(BF16).astype(F32)
            rest = rest - piece
            for _ in range(repeat):
                extra = jnp.where(row == place, piece, extra)
                place += 1
    first_ref[...] = jnp.concatenate([main_hi, main_hi, main_lo, extra], axis=0).astype(BF16)

    own_block = iota((wide, wide), 0) >> 6 == iota((wide, wide), 1) >> 6
    w2_rows = jnp.concatenate([w2_ref[...] * INV_TURN] * PARTS, axis=0)
    w2_full = jnp.where(own_block, tile_lanes(w2_rows), 0.0)
    w2_hi, w2_lo = split_two(w2_full)
    second_ref[0] = w2_hi
    second_ref[1] = w2_lo
    bias_ref[...] = tile_lanes(b2_ref[...]) * INV_TURN - 0.25

    lhs_rows = PARTS * OWN
    pick = iota((lhs_rows, CHANS), 1) == own_first + DEVS * (iota((lhs_rows, CHANS), 0) & (OWN - 1))
    chosen = jnp.where(pick, 1.0, 0.0).astype(BF16)
    keep = iota((lhs_rows, wide), 1) >> 6 == iota((lhs_rows, wide), 0) >> 3
    hi_part = jnp.concatenate([hi_ref[...]] * PARTS, axis=0)
    fix_part = jnp.concatenate([(fix_ref[...].astype(F32) * 2.0 ** (-11)).astype(BF16)] * PARTS, axis=0)
    third_ref[...] = jnp.concatenate(
        [jnp.where(keep, dot_nt(chosen, hi_part), 0.0), jnp.where(keep, dot_nt(chosen, fix_part), 0.0)], axis=0
    ).astype(BF16)
    env_ref[...] = jnp.broadcast_to(
        jnp.sum(jnp.where(pick, decay_ref[...], 0.0), axis=1, keepdims=True), (lhs_rows, 128)
    )


def filter_step(step, first_ref, second_ref, bias_ref, third_ref, env_ref, filt_ref):
    lane = iota((STEP, 128), 1)
    where_in = (iota((STEP, 128), 0) + step * STEP).astype(F32)
    freq = ((lane & 15) + 1).astype(F32)
    shift = jnp.where((lane & 16) == 0, 0.0, 0.25)
    value = turn_cos(where_in * freq * (1.0 / SEQ_LEN) - shift)
    value = jnp.where(lane < 96, value, where_in * (1.0 / QUARTER))
    value = jnp.where(lane < 100, value, 1.0)
    value = jnp.where(lane < 103, value, jnp.where(where_in > TOP - QUARTER * (PARTS - 1), 1.0, 0.0))
    value = jnp.where(lane < 106, value, 0.0)
    low = ((lane >= 32) & (lane < 64)) | (lane == 97) | (lane == 99)
    high = value.astype(BF16).astype(F32)
    feats = jnp.where(low, value - high, high).astype(BF16)
    one_hi, one_lo = split_two(turn_cos(dot(feats, first_ref[...])))
    turns = dot(one_hi, second_ref[0]) + dot(one_lo, second_ref[0]) + dot(one_hi, second_ref[1])
    two_hi, two_lo = split_two(turn_cos(turns + bias_ref[...]))
    both = dot_nt(third_ref[...], two_hi) + dot_nt(third_ref[...], two_lo)
    lhs_rows = PARTS * OWN
    shape = (lhs_rows, STEP)
    time = TOP - QUARTER * ((iota(shape, 0) >> 3)) - (iota(shape, 1) + step * STEP)
    time = jnp.where(time < 0, time + SEQ_LEN, time).astype(F32)
    rate = jnp.concatenate([env_ref[...]] * (STEP // 128), axis=1)
    envelope = jnp.exp(-rate * time) * jnp.sqrt(2.0 * rate + 1.0 / SEQ_LEN)
    filters = (both[:lhs_rows] + both[lhs_rows:]) * envelope
    for tile in range(STEP // 128):
        filt_ref[step * (STEP // 128) + tile] = filters[:, 128 * tile:128 * (tile + 1)]


def toeplitz_tiles(filt_ref, toep_ref):
    shape = (TAP, 128)
    ahead = iota(shape, 1) >= iota(shape, 0)
    inside = iota(shape, 1) <= iota(shape, 0) + (128 - TAP)
    per_part = QUARTER // 128

    def slanted(part, tile):
        taps = filt_ref[tile, pl.ds(pl.multiple_of(part * OWN, OWN), OWN), :]
        return tuple(
            pltpu.roll(jnp.broadcast_to(taps[chan:chan + 1], shape), 0, 1, stride=1, stride_axis=0)
            for chan in range(OWN)
        )

    def block(index, before):
        part = lax.div(index, DEPTH_PER_PART)
        first = lax.rem(index, DEPTH_PER_PART) * (DEPTH // 128)
        for sub in range(DEPTH // 128):
            now = slanted(part, first + sub)
            for chan in range(OWN):
                tile = jnp.where(ahead, now[chan], before[chan])
                if sub == DEPTH // 128 - 1:
                    tile = jnp.where(inside | (index < SEQ_LEN // DEPTH - 1), tile, 0.0)
                toep_ref[chan, pl.ds(pl.multiple_of(index * TAP, TAP), TAP), sub * 128:(sub + 1) * 128] = tile.astype(BF16)
            before = now
        return before

    lax.fori_loop(0, SEQ_LEN // DEPTH, block, slanted(PARTS - 1, per_part - 1))


def signal_windows(chan, recv_ref, rows_ref, win_ref):
    lane = iota((128, 128), 1)
    before = recv_ref[pl.ds(chan, 128, stride=OWN), :]
    after = recv_ref[pl.ds(chan + OWN, 128, stride=OWN), :]
    for sub in range(8):
        ahead = TAP * (sub + 1)
        value = after
        if ahead < 128:
            value = pltpu.roll(jnp.where(lane >= ahead, before, after), 128 - ahead, 1)
        rows_ref[pl.ds(56 + sub, 128, stride=8), :] = value
    win_ref[:, 0:128] = rows_ref[0:1072, :].astype(BF16)
    win_ref[:, 128:256] = rows_ref[8:1080, :].astype(BF16)


def convolve(chan, toep_ref, win_ref, conv_ref):
    sums = ([None] * 8, [None] * 8)
    for cols in range(4):
        window = jnp.concatenate(
            [win_ref[16 * deep + 256 * cols:16 * deep + 256 * (cols + 1), :] for deep in range(DEPTH // 256)], axis=1
        )
        part = dot_nt(toep_ref[chan, 64 * cols:256, :], window)
        for lag in range(16 - 4 * cols):
            row = TAP * (15 - lag - 4 * cols)
            for side in range(2):
                tile = 2 * cols + side + lag // 2
                if tile < 8:
                    piece = part[row:row + TAP, 128 * side:128 * (side + 1)]
                    old = sums[lag % 2][tile]
                    sums[lag % 2][tile] = piece if old is None else old + piece
    first_half = iota((TAP, 128), 1) < 64
    earlier = jnp.zeros((TAP, 128), F32)
    for tile in range(8):
        turned = pltpu.roll(sums[1][tile], 64, 1)
        conv_ref[tile, pl.ds(pl.multiple_of(chan * TAP, TAP), TAP), :] = sums[0][tile] + jnp.where(
            first_half, earlier, turned
        )
        earlier = turned


def block_kernel(sig_ref, gate_ref, skip_ref, decay_ref, w1_ref, b1_ref, w2_ref, b2_ref, hi_ref, fix_ref, wout_ref,
                 out_ref,
                 first_ref, second_ref, bias_ref, third_ref, env_ref, filt_ref, toep_ref, rows_ref, win_ref, conv_ref,
                 send_x, recv_x, send_y, recv_y, gated_ref, wide_ref, total_ref,
                 core_send, core_recv, far_send, far_recv,
                 wide_sem, x_send_sem, x_recv_sem, y_send_sem, y_recv_sem,
                 core_send_sem, core_recv_sem, far_send_sem, far_recv_sem):
    me = lax.axis_index("seq")
    group = lax.axis_index("ch")
    core = lax.rem(group, 2)
    chip = lax.div(group, 2)
    core_mate = chip * 2 + 1 - core
    far_mate = (1 - chip) * 2 + core

    barrier = pltpu.get_barrier_semaphore()

    @pl.loop(1, DEVS)
    def _(step):
        pl.semaphore_signal(barrier, inc=1, device_id={"seq": lax.rem(me + step, DEVS)}, device_id_type=MESH)

    for mate in (core_mate, far_mate):
        pl.semaphore_signal(barrier, inc=1, device_id={"ch": mate}, device_id_type=MESH)

    blocks = ((1 - chip) * 2 + 1 - core, far_mate, core_mate, group)
    loads = [
        pltpu.make_async_copy(
            wout_ref.at[:, pl.ds(pl.multiple_of(block * COLS, COLS), COLS)], wide_ref.at[slot], wide_sem.at[slot]
        )
        for slot, block in enumerate(blocks)
    ]
    for load in loads:
        load.start()

    for half in range(2):
        turned = sig_ref[128 * half:128 * (half + 1), :].astype(F32).T
        for chan in range(OWN):
            send_x[pl.ds(8 * half + chan, DEVS, stride=16), :] = turned[DEVS * chan:DEVS * (chan + 1), :]
    recv_x[0:OWN, :] = jnp.zeros((OWN, 128), F32)
    own_send = pl.ds(pl.multiple_of(me * 16, 16), 16)
    own_recv = pl.ds(pl.multiple_of(me * 16 + 8, 8), 16)
    recv_x[own_recv, :] = send_x[own_send, :]
    pl.semaphore_wait(barrier, DEVS + 1)

    @pl.loop(1, DEVS)
    def _(step):
        peer = lax.rem(me + step, DEVS)
        pltpu.make_async_remote_copy(
            src_ref=send_x.at[pl.ds(pl.multiple_of(peer * 16, 16), 16), :],
            dst_ref=recv_x.at[own_recv, :],
            send_sem=x_send_sem,
            recv_sem=x_recv_sem,
            device_id={"seq": peer},
            device_id_type=MESH,
        ).start()

    filter_weights(me, decay_ref, w1_ref, b1_ref, w2_ref, b2_ref, hi_ref, fix_ref,
                   first_ref, second_ref, bias_ref, third_ref, env_ref)

    @pl.loop(0, QUARTER // STEP)
    def _(step):
        filter_step(step, first_ref, second_ref, bias_ref, third_ref, env_ref, filt_ref)

    toeplitz_tiles(filt_ref, toep_ref)

    rows_ref[0:56, :] = jnp.zeros((56, 128), F32)
    many = pl.ds(0, (DEVS - 1) * 16)
    pltpu.make_async_copy(recv_x.at[many, :], recv_x.at[many, :], x_recv_sem).wait()

    @pl.loop(0, OWN, unroll=2)
    def _(chan):
        signal_windows(chan, recv_x, rows_ref, win_ref)
        convolve(chan, toep_ref, win_ref, conv_ref)

    for tile in range(8):
        turned = conv_ref[tile].T
        for peer in range(8):
            for quarter in range(4):
                place = 32 * tile + 4 * peer
                row = 16 * peer + 4 * quarter
                send_y[quarter, place:place + 4, :] = turned[row:row + 4, :]
    own_rows = pl.ds(pl.multiple_of(me * 4, 4), 4)
    for quarter in range(4):
        recv_y[quarter, own_rows, :] = send_y[quarter, own_rows, :]

        @pl.loop(1, DEVS)
        def _(step):
            peer = lax.rem(me + step, DEVS)
            pltpu.make_async_remote_copy(
                src_ref=send_y.at[quarter, pl.ds(pl.multiple_of(peer * 4, 4), 4), :],
                dst_ref=recv_y.at[quarter, own_rows, :],
                send_sem=y_send_sem.at[quarter],
                recv_sem=y_recv_sem.at[quarter],
                device_id={"seq": peer},
                device_id_type=MESH,
            ).start()

    def to_core(quarter, which):
        return pltpu.make_async_remote_copy(
            src_ref=core_send.at[quarter, which], dst_ref=core_recv.at[quarter, which],
            send_sem=core_send_sem.at[quarter, which], recv_sem=core_recv_sem.at[quarter, which],
            device_id={"ch": core_mate}, device_id_type=MESH,
        )

    def to_far(quarter):
        return pltpu.make_async_remote_copy(
            src_ref=far_send.at[quarter], dst_ref=far_recv.at[quarter],
            send_sem=far_send_sem.at[quarter], recv_sem=far_recv_sem.at[quarter],
            device_id={"ch": far_mate}, device_id_type=MESH,
        )

    for load in loads:
        load.wait()
    part_rows = pl.ds(0, (DEVS - 1) * 4)
    first_half = iota((16, 128), 1) < 64
    for quarter in range(4):
        pltpu.make_async_copy(
            recv_y.at[quarter, part_rows, :], recv_y.at[quarter, part_rows, :], y_recv_sem.at[quarter]
        ).wait()
        for pair in range(2):
            both = jnp.concatenate(
                [recv_y[quarter, pl.ds(2 * pair + side, DEVS, stride=4), :] for side in range(2)], axis=0
            ).T
            swapped = pltpu.roll(both, 64, 1)
            for two in range(OWN // 2):
                low = slice(32 * two, 32 * two + 16)
                high = slice(32 * two + 16, 32 * two + 32)
                lanes = slice(128 * two, 128 * (two + 1))
                for side, value in enumerate((
                    jnp.where(first_half, both[low], swapped[high]), jnp.where(first_half, swapped[low], both[high])
                )):
                    place = 16 * (2 * pair + side)
                    rows = slice(64 * quarter + place, 64 * quarter + place + 16)
                    gated_ref[place:place + 16, lanes] = (
                        gate_ref[rows, lanes].astype(F32)
                        * (value + skip_ref[:, lanes] * sig_ref[rows, lanes].astype(F32))
                    ).astype(BF16)
        core_send[quarter, 0] = dot(gated_ref[...], wide_ref[0])
        to_core(quarter, 0).start()
        far_send[quarter] = dot(gated_ref[...], wide_ref[1])
        to_core(quarter, 0).wait_recv()
        far_send[quarter] += core_recv[quarter, 0]
        to_far(quarter).start()
        core_send[quarter, 1] = dot(gated_ref[...], wide_ref[2])
        to_core(quarter, 1).start()
        total_ref[quarter] = dot(gated_ref[...], wide_ref[3])
    for quarter in range(4):
        to_core(quarter, 1).wait_recv()
        to_far(quarter).wait_recv()
        out_ref[64 * quarter:64 * (quarter + 1), :] = (
            total_ref[quarter] + core_recv[quarter, 1] + far_recv[quarter]
        ).astype(BF16)

    pltpu.make_async_copy(send_x.at[many, :], send_x.at[many, :], x_send_sem).wait()
    for quarter in range(4):
        pltpu.make_async_copy(
            send_y.at[quarter, part_rows, :], send_y.at[quarter, part_rows, :], y_send_sem.at[quarter]
        ).wait()
        for which in range(2):
            to_core(quarter, which).wait_send()
        to_far(quarter).wait_send()


def shards(signal, gate_in, skip_gain, decay, pos_weight1, pos_bias1, pos_weight2, pos_bias2, filt_hi, filt_fix,
           out_weight):
    vmem = pl.BlockSpec(memory_space=pltpu.VMEM)
    wide = PARTS * HID
    return pl.pallas_call(
        block_kernel,
        out_shape=jax.ShapeDtypeStruct((ROWS, COLS), BF16),
        in_specs=[vmem] * 10 + [pl.BlockSpec(memory_space=pl.ANY)],
        out_specs=vmem,
        scratch_shapes=[
            pltpu.VMEM((128, wide), BF16),
            pltpu.VMEM((2, wide, wide), BF16),
            pltpu.VMEM((1, wide), F32),
            pltpu.VMEM((2 * PARTS * OWN, wide), BF16),
            pltpu.VMEM((PARTS * OWN, 128), F32),
            pltpu.VMEM((QUARTER // 128, PARTS * OWN, 128), F32),
            pltpu.VMEM((OWN, SEQ_LEN // DEPTH * TAP, DEPTH), BF16),
            pltpu.VMEM((1088, 128), F32),
            pltpu.VMEM((1072, 256), BF16),
            pltpu.VMEM((8, 128, 128), F32),
            pltpu.VMEM((DEVS * 16, 128), F32),
            pltpu.VMEM((DEVS * 16 + 8, 128), F32),
            pltpu.VMEM((4, DEVS * 4, 128), F32),
            pltpu.VMEM((4, DEVS * 4, 128), F32),
            pltpu.VMEM((64, CHANS), BF16),
            pltpu.VMEM((4, CHANS, COLS), BF16),
            pltpu.VMEM((4, 64, COLS), F32),
            pltpu.VMEM((4, 2, 64, COLS), F32),
            pltpu.VMEM((4, 2, 64, COLS), F32),
            pltpu.VMEM((4, 64, COLS), F32),
            pltpu.VMEM((4, 64, COLS), F32),
            pltpu.SemaphoreType.DMA((4,)),
            pltpu.SemaphoreType.DMA,
            pltpu.SemaphoreType.DMA,
            pltpu.SemaphoreType.DMA((4,)),
            pltpu.SemaphoreType.DMA((4,)),
            pltpu.SemaphoreType.DMA((4, 2)),
            pltpu.SemaphoreType.DMA((4, 2)),
            pltpu.SemaphoreType.DMA((4,)),
            pltpu.SemaphoreType.DMA((4,)),
        ],
        compiler_params=pltpu.CompilerParams(
            collective_id=0, has_side_effects=True, vmem_limit_bytes=56 * 2**20
        ),
        name="hyena_block",
    )(
        signal, gate_in, skip_gain[None, :], decay[None, :], pos_weight1, pos_bias1[None, :], pos_weight2,
        pos_bias2[None, :], filt_hi, filt_fix, out_weight,
    )


def solution(mesh):
    return jax.shard_map(
        shards,
        mesh=mesh,
        in_specs=(
            P("seq", "ch"), P("seq", "ch"), P("ch"), P("ch"), P(), P(), P(), P(), P(None, "ch"), P(None, "ch"),
            P("ch", None),
        ),
        out_specs=P("seq", "ch"),
        check_vma=False,
    )
```

```python
import math

import jax
import jax.numpy as jnp
from jax import lax
from jax.experimental import pallas as pl
from jax.experimental.pallas import tpu as pltpu
from jax.sharding import PartitionSpec as P

F32 = jnp.float32
BF16 = jnp.bfloat16
MESH = pl.DeviceIdType.MESH

SEQ_LEN = 16384
DEVS = 64
ROWS = 256
CHANS = 512
OWN = 8
SUB = 4
HID = 64
PARTS = 4
QUARTER = SEQ_LEN // PARTS
STEP = 1024
TAP = 16
DEPTH = 1024
DEPTH_PER_PART = QUARTER // DEPTH
TOP = SEQ_LEN - TAP
COLS = 1024
INV_TURN = 1.0 / (2.0 * math.pi)
COS_POLY = (6.283185159611168, -41.34165492934356, 81.60099819261757, -76.54965682073457, 39.53581371237487)


def turn_cos(turns):
    near = turns - jnp.round(turns)
    arg = 0.25 - jnp.abs(near)
    square = arg * arg
    c0, c1, c2, c3, c4 = COS_POLY
    return arg * (c0 + square * (c1 + square * (c2 + square * (c3 + square * c4))))


def split_two(value):
    high = value.astype(BF16)
    return high, (value - high.astype(F32)).astype(BF16)


def dot(left, right):
    return jnp.dot(left, right, preferred_element_type=F32)


def dot_nt(left, right):
    return lax.dot_general(left, right, (((1,), (1,)), ((), ())), preferred_element_type=F32)


def tile_lanes(value):
    return jnp.concatenate([value] * PARTS, axis=1)


def iota(shape, axis):
    return lax.broadcasted_iota(jnp.int32, shape, axis)


def filter_weights(own_first, decay_ref, w1_ref, b1_ref, w2_ref, b2_ref, hi_ref, fix_ref,
                   first_ref, second_ref, bias_ref, third_ref, env_ref):
    wide = PARTS * HID
    part = iota((16, wide), 1) >> 6
    freq = (iota((16, wide), 0) + 1).astype(F32)
    turns = freq * (TOP - QUARTER * part).astype(F32) * (1.0 / SEQ_LEN)
    cos_top, sin_top = turn_cos(turns), turn_cos(turns - 0.25)
    w_lin = tile_lanes(w1_ref[0:1, :]) * INV_TURN
    w_cos = tile_lanes(w1_ref[1:17, :]) * INV_TURN
    w_sin = tile_lanes(w1_ref[17:33, :]) * INV_TURN
    main = jnp.concatenate(
        [w_cos * cos_top + w_sin * sin_top, w_cos * sin_top - w_sin * cos_top], axis=0
    )
    main_hi = main.astype(BF16).astype(F32)
    main_lo = main - main_hi
    part_row = iota((1, wide), 1) >> 6
    top_row = (TOP - QUARTER * part_row).astype(F32) * (1.0 / SEQ_LEN)
    slope = -w_lin / PARTS
    const = w_lin * top_row + tile_lanes(b1_ref[...]) * INV_TURN - 0.25
    wrap = jnp.where(part_row == PARTS - 1, w_lin, 0.0)
    extra = jnp.zeros((32, wide), F32)
    row = iota((32, wide), 0)
    place = 0
    for value, pieces, repeat in ((slope, 2, 2), (const, 3, 1), (wrap, 3, 1)):
        rest = value
        for _ in range(pieces):
            piece = rest.astype(BF16).astype(F32)
            rest = rest - piece
            for _ in range(repeat):
                extra = jnp.where(row == place, piece, extra)
                place += 1
    first_ref[...] = jnp.concatenate([main_hi, main_hi, main_lo, extra], axis=0).astype(BF16)

    own_block = iota((wide, wide), 0) >> 6 == iota((wide, wide), 1) >> 6
    w2_rows = jnp.concatenate([w2_ref[...] * INV_TURN] * PARTS, axis=0)
    w2_full = jnp.where(own_block, tile_lanes(w2_rows), 0.0)
    w2_hi, w2_lo = split_two(w2_full)
    second_ref[0] = w2_hi
    second_ref[1] = w2_lo
    bias_ref[...] = tile_lanes(b2_ref[...]) * INV_TURN - 0.25

    lhs_rows = PARTS * OWN
    pick = iota((lhs_rows, CHANS), 1) == own_first + DEVS * (iota((lhs_rows, CHANS), 0) & (OWN - 1))
    chosen = jnp.where(pick, 1.0, 0.0).astype(BF16)
    keep = iota((lhs_rows, wide), 1) >> 6 == iota((lhs_rows, wide), 0) >> 3
    hi_part = jnp.concatenate([hi_ref[...]] * PARTS, axis=0)
    fix_part = jnp.concatenate([(fix_ref[...].astype(F32) * 2.0 ** (-11)).astype(BF16)] * PARTS, axis=0)
    third_ref[...] = jnp.concatenate(
        [jnp.where(keep, dot_nt(chosen, hi_part), 0.0), jnp.where(keep, dot_nt(chosen, fix_part), 0.0)], axis=0
    ).astype(BF16)
    env_ref[...] = jnp.broadcast_to(
        jnp.sum(jnp.where(pick, decay_ref[...], 0.0), axis=1, keepdims=True), (lhs_rows, 128)
    )


def filter_step(step, first_ref, second_ref, bias_ref, third_ref, env_ref, filt_ref):
    lane = iota((STEP, 128), 1)
    where_in = (iota((STEP, 128), 0) + step * STEP).astype(F32)
    freq = ((lane & 15) + 1).astype(F32)
    shift = jnp.where((lane & 16) == 0, 0.0, 0.25)
    value = turn_cos(where_in * freq * (1.0 / SEQ_LEN) - shift)
    value = jnp.where(lane < 96, value, where_in * (1.0 / QUARTER))
    value = jnp.where(lane < 100, value, 1.0)
    value = jnp.where(lane < 103, value, jnp.where(where_in > TOP - QUARTER * (PARTS - 1), 1.0, 0.0))
    value = jnp.where(lane < 106, value, 0.0)
    low = ((lane >= 32) & (lane < 64)) | (lane == 97) | (lane == 99)
    high = value.astype(BF16).astype(F32)
    feats = jnp.where(low, value - high, high).astype(BF16)
    one_hi, one_lo = split_two(turn_cos(dot(feats, first_ref[...])))
    turns = dot(one_hi, second_ref[0]) + dot(one_lo, second_ref[0]) + dot(one_hi, second_ref[1])
    two_hi, two_lo = split_two(turn_cos(turns + bias_ref[...]))
    both = dot_nt(third_ref[...], two_hi) + dot_nt(third_ref[...], two_lo)
    lhs_rows = PARTS * OWN
    shape = (lhs_rows, STEP)
    time = TOP - QUARTER * ((iota(shape, 0) >> 3)) - (iota(shape, 1) + step * STEP)
    time = jnp.where(time < 0, time + SEQ_LEN, time).astype(F32)
    rate = jnp.concatenate([env_ref[...]] * (STEP // 128), axis=1)
    envelope = jnp.exp(-rate * time) * jnp.sqrt(2.0 * rate + 1.0 / SEQ_LEN)
    filters = (both[:lhs_rows] + both[lhs_rows:]) * envelope
    for tile in range(STEP // 128):
        filt_ref[step * (STEP // 128) + tile] = filters[:, 128 * tile:128 * (tile + 1)]


def toeplitz_tiles(filt_ref, toep_ref):
    shape = (TAP, 128)
    ahead = iota(shape, 1) >= iota(shape, 0)
    inside = iota(shape, 1) <= iota(shape, 0) + (128 - TAP)
    per_part = QUARTER // 128

    def slanted(part, tile):
        taps = filt_ref[tile, pl.ds(pl.multiple_of(part * OWN, OWN), OWN), :]
        return tuple(
            pltpu.roll(jnp.broadcast_to(taps[chan:chan + 1], shape), 0, 1, stride=1, stride_axis=0)
            for chan in range(OWN)
        )

    def block(index, before):
        part = lax.div(index, DEPTH_PER_PART)
        first = lax.rem(index, DEPTH_PER_PART) * (DEPTH // 128)
        for sub in range(DEPTH // 128):
            now = slanted(part, first + sub)
            for chan in range(OWN):
                tile = jnp.where(ahead, now[chan], before[chan])
                if sub == DEPTH // 128 - 1:
                    tile = jnp.where(inside | (index < SEQ_LEN // DEPTH - 1), tile, 0.0)
                toep_ref[chan, pl.ds(pl.multiple_of(index * TAP, TAP), TAP), sub * 128:(sub + 1) * 128] = tile.astype(BF16)
            before = now
        return before

    lax.fori_loop(0, SEQ_LEN // DEPTH, block, slanted(PARTS - 1, per_part - 1))


def signal_windows(chan, recv_ref, rows_ref, win_ref):
    lane = iota((128, 128), 1)
    before = recv_ref[pl.ds(SUB + chan, 128, stride=SUB), :]
    after = recv_ref[pl.ds(2 * SUB + chan, 128, stride=SUB), :]
    for sub in range(8):
        ahead = TAP * (sub + 1)
        value = after
        if ahead < 128:
            value = pltpu.roll(jnp.where(lane >= ahead, before, after), 128 - ahead, 1)
        rows_ref[pl.ds(56 + sub, 128, stride=8), :] = value
    win_ref[:, 0:128] = rows_ref[0:1072, :].astype(BF16)
    win_ref[:, 128:256] = rows_ref[8:1080, :].astype(BF16)


def convolve(chan, toep_ref, win_ref, conv_ref):
    sums = ([None] * 8, [None] * 8)
    for cols in range(4):
        window = jnp.concatenate(
            [win_ref[16 * deep + 256 * cols:16 * deep + 256 * (cols + 1), :] for deep in range(DEPTH // 256)], axis=1
        )
        part = dot_nt(toep_ref[chan, 64 * cols:256, :], window)
        for lag in range(16 - 4 * cols):
            row = TAP * (15 - lag - 4 * cols)
            for side in range(2):
                tile = 2 * cols + side + lag // 2
                if tile < 8:
                    piece = part[row:row + TAP, 128 * side:128 * (side + 1)]
                    old = sums[lag % 2][tile]
                    sums[lag % 2][tile] = piece if old is None else old + piece
    first_half = iota((TAP, 128), 1) < 64
    earlier = jnp.zeros((TAP, 128), F32)
    for tile in range(8):
        turned = pltpu.roll(sums[1][tile], 64, 1)
        conv_ref[tile, pl.ds(pl.multiple_of(chan * TAP, TAP), TAP), :] = sums[0][tile] + jnp.where(
            first_half, earlier, turned
        )
        earlier = turned


def block_kernel(sig_ref, gate_ref, skip_ref, decay_ref, w1_ref, b1_ref, w2_ref, b2_ref, hi_ref, fix_ref, wout_ref,
                 out_ref,
                 first_ref, second_ref, bias_ref, third_ref, env_ref, filt_ref, toep_ref, rows_ref, win_ref, conv_ref,
                 send_x, recv_x, send_y, recv_y, gated_ref, wide_ref, total_ref, mixed_ref,
                 core_send, core_recv, far_send, far_recv,
                 wide_sem, x_send_sem, x_recv_sem, y_send_sem, y_recv_sem,
                 core_send_sem, core_recv_sem, far_send_sem, far_recv_sem, out_sem):
    me = lax.axis_index("seq")
    group = lax.axis_index("ch")
    core = lax.rem(group, 2)
    chip = lax.div(group, 2)
    core_mate = chip * 2 + 1 - core
    far_mate = (1 - chip) * 2 + core

    barrier = pltpu.get_barrier_semaphore()

    @pl.loop(1, DEVS)
    def _(step):
        pl.semaphore_signal(barrier, inc=1, device_id={"seq": lax.rem(me + step, DEVS)}, device_id_type=MESH)

    for mate in (core_mate, far_mate):
        pl.semaphore_signal(barrier, inc=1, device_id={"ch": mate}, device_id_type=MESH)

    blocks = ((1 - chip) * 2 + 1 - core, far_mate, core_mate, group)
    loads = [
        pltpu.make_async_copy(
            wout_ref.at[:, pl.ds(pl.multiple_of(block * COLS, COLS), COLS)], wide_ref.at[slot], wide_sem.at[slot]
        )
        for slot, block in enumerate(blocks)
    ]
    for load in loads:
        load.start()

    for half in range(2):
        turned = sig_ref[128 * half:128 * (half + 1), :].astype(F32).T
        for chan in range(OWN):
            send_x[chan // SUB, pl.ds(SUB * half + chan % SUB, DEVS, stride=8), :] = (
                turned[DEVS * chan:DEVS * (chan + 1), :]
            )
    own_send = pl.ds(pl.multiple_of(me * 8, 8), 8)
    own_recv = pl.ds(pl.multiple_of(me * 8 + 8, 8), 8)
    for group_num in range(2):
        recv_x[group_num, 0:8, :] = jnp.zeros((8, 128), F32)
        recv_x[group_num, own_recv, :] = send_x[group_num, own_send, :]
    pl.semaphore_wait(barrier, DEVS + 1)

    for group_num in range(2):

        @pl.loop(1, DEVS)
        def _(step):
            peer = lax.rem(me + step, DEVS)
            pltpu.make_async_remote_copy(
                src_ref=send_x.at[group_num, pl.ds(pl.multiple_of(peer * 8, 8), 8), :],
                dst_ref=recv_x.at[group_num, own_recv, :],
                send_sem=x_send_sem.at[group_num],
                recv_sem=x_recv_sem.at[group_num],
                device_id={"seq": peer},
                device_id_type=MESH,
            ).start()

    filter_weights(me, decay_ref, w1_ref, b1_ref, w2_ref, b2_ref, hi_ref, fix_ref,
                   first_ref, second_ref, bias_ref, third_ref, env_ref)

    @pl.loop(0, QUARTER // STEP)
    def _(step):
        filter_step(step, first_ref, second_ref, bias_ref, third_ref, env_ref, filt_ref)

    toeplitz_tiles(filt_ref, toep_ref)

    rows_ref[0:56, :] = jnp.zeros((56, 128), F32)
    many = pl.ds(0, (DEVS - 1) * 8)
    for group_num in range(2):
        pltpu.make_async_copy(
            recv_x.at[group_num, many, :], recv_x.at[group_num, many, :], x_recv_sem.at[group_num]
        ).wait()

        @pl.loop(0, SUB, unroll=2)
        def _(chan):
            signal_windows(chan, recv_x.at[group_num], rows_ref, win_ref)
            convolve(group_num * SUB + chan, toep_ref, win_ref, conv_ref)

    for tile in range(8):
        turned = conv_ref[tile].T
        for peer in range(8):
            for quarter in range(4):
                place = 32 * tile + 4 * peer
                row = 16 * peer + 4 * quarter
                send_y[quarter, place:place + 4, :] = turned[row:row + 4, :]
    own_rows = pl.ds(pl.multiple_of(me * 4, 4), 4)
    for quarter in range(4):
        recv_y[quarter, own_rows, :] = send_y[quarter, own_rows, :]

        @pl.loop(1, DEVS)
        def _(step):
            peer = lax.rem(me + step, DEVS)
            pltpu.make_async_remote_copy(
                src_ref=send_y.at[quarter, pl.ds(pl.multiple_of(peer * 4, 4), 4), :],
                dst_ref=recv_y.at[quarter, own_rows, :],
                send_sem=y_send_sem.at[quarter],
                recv_sem=y_recv_sem.at[quarter],
                device_id={"seq": peer},
                device_id_type=MESH,
            ).start()

    def to_core(quarter, which):
        return pltpu.make_async_remote_copy(
            src_ref=core_send.at[quarter, which], dst_ref=core_recv.at[quarter, which],
            send_sem=core_send_sem.at[quarter, which], recv_sem=core_recv_sem.at[quarter, which],
            device_id={"ch": core_mate}, device_id_type=MESH,
        )

    def to_far(quarter):
        return pltpu.make_async_remote_copy(
            src_ref=far_send.at[quarter], dst_ref=far_recv.at[quarter],
            send_sem=far_send_sem.at[quarter], recv_sem=far_recv_sem.at[quarter],
            device_id={"ch": far_mate}, device_id_type=MESH,
        )

    def to_out(quarter):
        return pltpu.make_async_copy(
            mixed_ref.at[quarter], out_ref.at[64 * quarter:64 * (quarter + 1), :], out_sem.at[quarter]
        )

    for load in loads:
        load.wait()
    part_rows = pl.ds(0, (DEVS - 1) * 4)
    first_half = iota((16, 128), 1) < 64
    for quarter in range(4):
        pltpu.make_async_copy(
            recv_y.at[quarter, part_rows, :], recv_y.at[quarter, part_rows, :], y_recv_sem.at[quarter]
        ).wait()
        for pair in range(2):
            both = jnp.concatenate(
                [recv_y[quarter, pl.ds(2 * pair + side, DEVS, stride=4), :] for side in range(2)], axis=0
            ).T
            swapped = pltpu.roll(both, 64, 1)
            for two in range(OWN // 2):
                low = slice(32 * two, 32 * two + 16)
                high = slice(32 * two + 16, 32 * two + 32)
                lanes = slice(128 * two, 128 * (two + 1))
                for side, value in enumerate((
                    jnp.where(first_half, both[low], swapped[high]), jnp.where(first_half, swapped[low], both[high])
                )):
                    place = 16 * (2 * pair + side)
                    rows = slice(64 * quarter + place, 64 * quarter + place + 16)
                    gated_ref[place:place + 16, lanes] = (
                        gate_ref[rows, lanes].astype(F32)
                        * (value + skip_ref[:, lanes] * sig_ref[rows, lanes].astype(F32))
                    ).astype(BF16)
        core_send[quarter, 0] = dot(gated_ref[...], wide_ref[0])
        to_core(quarter, 0).start()
        far_send[quarter] = dot(gated_ref[...], wide_ref[1])
        to_core(quarter, 0).wait_recv()
        far_send[quarter] += core_recv[quarter, 0]
        to_far(quarter).start()
        core_send[quarter, 1] = dot(gated_ref[...], wide_ref[2])
        to_core(quarter, 1).start()
        total_ref[quarter] = dot(gated_ref[...], wide_ref[3])
    for quarter in range(4):
        to_core(quarter, 1).wait_recv()
        to_far(quarter).wait_recv()
        mixed_ref[quarter] = (total_ref[quarter] + core_recv[quarter, 1] + far_recv[quarter]).astype(BF16)
        to_out(quarter).start()
    for quarter in range(4):
        to_out(quarter).wait()

    for group_num in range(2):
        pltpu.make_async_copy(
            send_x.at[group_num, many, :], send_x.at[group_num, many, :], x_send_sem.at[group_num]
        ).wait()
    for quarter in range(4):
        pltpu.make_async_copy(
            send_y.at[quarter, part_rows, :], send_y.at[quarter, part_rows, :], y_send_sem.at[quarter]
        ).wait()
        for which in range(2):
            to_core(quarter, which).wait_send()
        to_far(quarter).wait_send()


def shards(signal, gate_in, skip_gain, decay, pos_weight1, pos_bias1, pos_weight2, pos_bias2, filt_hi, filt_fix,
           out_weight):
    vmem = pl.BlockSpec(memory_space=pltpu.VMEM)
    wide = PARTS * HID
    return pl.pallas_call(
        block_kernel,
        out_shape=jax.ShapeDtypeStruct((ROWS, COLS), BF16),
        in_specs=[vmem] * 10 + [pl.BlockSpec(memory_space=pl.ANY)],
        out_specs=pl.BlockSpec(memory_space=pl.ANY),
        scratch_shapes=[
            pltpu.VMEM((128, wide), BF16),
            pltpu.VMEM((2, wide, wide), BF16),
            pltpu.VMEM((1, wide), F32),
            pltpu.VMEM((2 * PARTS * OWN, wide), BF16),
            pltpu.VMEM((PARTS * OWN, 128), F32),
            pltpu.VMEM((QUARTER // 128, PARTS * OWN, 128), F32),
            pltpu.VMEM((OWN, SEQ_LEN // DEPTH * TAP, DEPTH), BF16),
            pltpu.VMEM((1088, 128), F32),
            pltpu.VMEM((1072, 256), BF16),
            pltpu.VMEM((8, 128, 128), F32),
            pltpu.VMEM((2, DEVS * 8, 128), F32),
            pltpu.VMEM((2, DEVS * 8 + 8, 128), F32),
            pltpu.VMEM((4, DEVS * 4, 128), F32),
            pltpu.VMEM((4, DEVS * 4, 128), F32),
            pltpu.VMEM((64, CHANS), BF16),
            pltpu.VMEM((4, CHANS, COLS), BF16),
            pltpu.VMEM((4, 64, COLS), F32),
            pltpu.VMEM((4, 64, COLS), BF16),
            pltpu.VMEM((4, 2, 64, COLS), F32),
            pltpu.VMEM((4, 2, 64, COLS), F32),
            pltpu.VMEM((4, 64, COLS), F32),
            pltpu.VMEM((4, 64, COLS), F32),
            pltpu.SemaphoreType.DMA((4,)),
            pltpu.SemaphoreType.DMA((2,)),
            pltpu.SemaphoreType.DMA((2,)),
            pltpu.SemaphoreType.DMA((4,)),
            pltpu.SemaphoreType.DMA((4,)),
            pltpu.SemaphoreType.DMA((4, 2)),
            pltpu.SemaphoreType.DMA((4, 2)),
            pltpu.SemaphoreType.DMA((4,)),
            pltpu.SemaphoreType.DMA((4,)),
            pltpu.SemaphoreType.DMA((4,)),
        ],
        compiler_params=pltpu.CompilerParams(
            collective_id=0, has_side_effects=True, vmem_limit_bytes=56 * 2**20
        ),
        name="hyena_block",
    )(
        signal, gate_in, skip_gain[None, :], decay[None, :], pos_weight1, pos_bias1[None, :], pos_weight2,
        pos_bias2[None, :], filt_hi, filt_fix, out_weight,
    )


def solution(mesh):
    return jax.shard_map(
        shards,
        mesh=mesh,
        in_specs=(
            P("seq", "ch"), P("seq", "ch"), P("ch"), P("ch"), P(), P(), P(), P(), P(None, "ch"), P(None, "ch"),
            P("ch", None),
        ),
        out_specs=P("seq", "ch"),
        check_vma=False,
    )
```

```python
import math

import jax
import jax.numpy as jnp
from jax import lax
from jax.experimental import pallas as pl
from jax.experimental.pallas import tpu as pltpu
from jax.sharding import PartitionSpec as P

F32 = jnp.float32
BF16 = jnp.bfloat16
MESH = pl.DeviceIdType.MESH

SEQ_LEN = 16384
DEVS = 64
ROWS = 256
CHANS = 512
OWN = 8
SUB = 4
HID = 64
PARTS = 4
QUARTER = SEQ_LEN // PARTS
STEP = 1024
TAP = 16
DEPTH = 1024
DEPTH_PER_PART = QUARTER // DEPTH
TOP = SEQ_LEN - TAP
COLS = 1024
INV_TURN = 1.0 / (2.0 * math.pi)
COS_POLY = (6.283185159611168, -41.34165492934356, 81.60099819261757, -76.54965682073457, 39.53581371237487)


def turn_cos(turns):
    near = turns - jnp.round(turns)
    arg = 0.25 - jnp.abs(near)
    square = arg * arg
    c0, c1, c2, c3, c4 = COS_POLY
    return arg * (c0 + square * (c1 + square * (c2 + square * (c3 + square * c4))))


def split_two(value):
    high = value.astype(BF16)
    return high, (value - high.astype(F32)).astype(BF16)


def dot(left, right):
    return jnp.dot(left, right, preferred_element_type=F32)


def dot_nt(left, right):
    return lax.dot_general(left, right, (((1,), (1,)), ((), ())), preferred_element_type=F32)


def tile_lanes(value):
    return jnp.concatenate([value] * PARTS, axis=1)


def iota(shape, axis):
    return lax.broadcasted_iota(jnp.int32, shape, axis)


def filter_weights(own_first, decay_ref, w1_ref, b1_ref, w2_ref, b2_ref, hi_ref, fix_ref,
                   first_ref, second_ref, bias_ref, third_ref, env_ref):
    wide = PARTS * HID
    part = iota((16, wide), 1) >> 6
    freq = (iota((16, wide), 0) + 1).astype(F32)
    turns = freq * (TOP - QUARTER * part).astype(F32) * (1.0 / SEQ_LEN)
    cos_top, sin_top = turn_cos(turns), turn_cos(turns - 0.25)
    w_lin = tile_lanes(w1_ref[0:1, :]) * INV_TURN
    w_cos = tile_lanes(w1_ref[1:17, :]) * INV_TURN
    w_sin = tile_lanes(w1_ref[17:33, :]) * INV_TURN
    main = jnp.concatenate(
        [w_cos * cos_top + w_sin * sin_top, w_cos * sin_top - w_sin * cos_top], axis=0
    )
    main_hi = main.astype(BF16).astype(F32)
    main_lo = main - main_hi
    part_row = iota((1, wide), 1) >> 6
    top_row = (TOP - QUARTER * part_row).astype(F32) * (1.0 / SEQ_LEN)
    slope = -w_lin / PARTS
    const = w_lin * top_row + tile_lanes(b1_ref[...]) * INV_TURN - 0.25
    wrap = jnp.where(part_row == PARTS - 1, w_lin, 0.0)
    extra = jnp.zeros((32, wide), F32)
    row = iota((32, wide), 0)
    place = 0
    for value, pieces, repeat in ((slope, 2, 2), (const, 3, 1), (wrap, 3, 1)):
        rest = value
        for _ in range(pieces):
            piece = rest.astype(BF16).astype(F32)
            rest = rest - piece
            for _ in range(repeat):
                extra = jnp.where(row == place, piece, extra)
                place += 1
    first_ref[...] = jnp.concatenate([main_hi, main_hi, main_lo, extra], axis=0).astype(BF16)

    own_block = iota((wide, wide), 0) >> 6 == iota((wide, wide), 1) >> 6
    w2_rows = jnp.concatenate([w2_ref[...] * INV_TURN] * PARTS, axis=0)
    w2_full = jnp.where(own_block, tile_lanes(w2_rows), 0.0)
    w2_hi, w2_lo = split_two(w2_full)
    second_ref[0] = w2_hi
    second_ref[1] = w2_lo
    bias_ref[...] = tile_lanes(b2_ref[...]) * INV_TURN - 0.25

    lhs_rows = PARTS * OWN
    pick = iota((lhs_rows, CHANS), 1) == own_first + DEVS * (iota((lhs_rows, CHANS), 0) & (OWN - 1))
    chosen = jnp.where(pick, 1.0, 0.0).astype(BF16)
    keep = iota((lhs_rows, wide), 1) >> 6 == iota((lhs_rows, wide), 0) >> 3
    hi_part = jnp.concatenate([hi_ref[...]] * PARTS, axis=0)
    fix_part = jnp.concatenate([(fix_ref[...].astype(F32) * 2.0 ** (-11)).astype(BF16)] * PARTS, axis=0)
    third_ref[...] = jnp.concatenate(
        [jnp.where(keep, dot_nt(chosen, hi_part), 0.0), jnp.where(keep, dot_nt(chosen, fix_part), 0.0)], axis=0
    ).astype(BF16)
    env_ref[...] = jnp.broadcast_to(
        jnp.sum(jnp.where(pick, decay_ref[...], 0.0), axis=1, keepdims=True), (lhs_rows, 128)
    )


def filter_step(step, first_ref, second_ref, bias_ref, third_ref, env_ref, filt_ref):
    lane = iota((1, 128), 1)
    where_in = (iota((STEP, 128), 0) + step * STEP).astype(F32)
    rate = ((lane & 15) + 1).astype(F32) * (1.0 / SEQ_LEN)
    shift = jnp.where((lane & 16) == 0, 0.0, 0.25)
    slope = jnp.where(lane < 100, 1.0 / QUARTER, 0.0)
    start = jnp.where((lane >= 100) & (lane < 103), 1.0, 0.0)
    turn = jnp.where((lane >= 103) & (lane < 106), float(TOP - QUARTER * (PARTS - 1)), float(SEQ_LEN))
    value = jnp.where(lane < 96, turn_cos(where_in * rate - shift), where_in * slope + start)
    value = jnp.where(where_in > turn, 1.0, value)
    low = ((lane >= 32) & (lane < 64)) | (lane == 97) | (lane == 99)
    high = value.astype(BF16).astype(F32)
    feats = jnp.where(low, value - high, high).astype(BF16)
    one_hi, one_lo = split_two(turn_cos(dot(feats, first_ref[...])))
    turns = dot(one_hi, second_ref[0]) + dot(one_lo, second_ref[0]) + dot(one_hi, second_ref[1])
    two_hi, two_lo = split_two(turn_cos(turns + bias_ref[...]))
    both = dot_nt(third_ref[...], two_hi) + dot_nt(third_ref[...], two_lo)
    lhs_rows = PARTS * OWN
    shape = (lhs_rows, STEP)
    time = TOP - QUARTER * ((iota(shape, 0) >> 3)) - (iota(shape, 1) + step * STEP)
    time = jnp.where(time < 0, time + SEQ_LEN, time).astype(F32)
    rate = jnp.concatenate([env_ref[...]] * (STEP // 128), axis=1)
    envelope = jnp.exp(-rate * time) * jnp.sqrt(2.0 * rate + 1.0 / SEQ_LEN)
    filters = (both[:lhs_rows] + both[lhs_rows:]) * envelope
    for tile in range(STEP // 128):
        filt_ref[step * (STEP // 128) + tile] = filters[:, 128 * tile:128 * (tile + 1)]


def toeplitz_tiles(filt_ref, toep_ref):
    shape = (TAP, 128)
    ahead = iota(shape, 1) >= iota(shape, 0)
    inside = iota(shape, 1) <= iota(shape, 0) + (128 - TAP)
    per_part = QUARTER // 128

    def slanted(part, tile):
        taps = filt_ref[tile, pl.ds(pl.multiple_of(part * OWN, OWN), OWN), :]
        return tuple(
            pltpu.roll(jnp.broadcast_to(taps[chan:chan + 1], shape), 0, 1, stride=1, stride_axis=0)
            for chan in range(OWN)
        )

    def block(index, before):
        part = lax.div(index, DEPTH_PER_PART)
        first = lax.rem(index, DEPTH_PER_PART) * (DEPTH // 128)
        for sub in range(DEPTH // 128):
            now = slanted(part, first + sub)
            for chan in range(OWN):
                tile = jnp.where(ahead, now[chan], before[chan])
                if sub == DEPTH // 128 - 1:
                    tile = jnp.where(inside | (index < SEQ_LEN // DEPTH - 1), tile, 0.0)
                toep_ref[chan, pl.ds(pl.multiple_of(index * TAP, TAP), TAP), sub * 128:(sub + 1) * 128] = tile.astype(BF16)
            before = now
        return before

    lax.fori_loop(0, SEQ_LEN // DEPTH, block, slanted(PARTS - 1, per_part - 1))


def signal_windows(chan, recv_ref, rows_ref, win_ref):
    lane = iota((128, 128), 1)
    before = recv_ref[pl.ds(SUB + chan, 128, stride=SUB), :]
    after = recv_ref[pl.ds(2 * SUB + chan, 128, stride=SUB), :]
    for sub in range(8):
        ahead = TAP * (sub + 1)
        value = after
        if ahead < 128:
            value = pltpu.roll(jnp.where(lane >= ahead, before, after), 128 - ahead, 1)
        rows_ref[pl.ds(56 + sub, 128, stride=8), :] = value
    win_ref[:, 0:128] = rows_ref[0:1072, :].astype(BF16)
    win_ref[:, 128:256] = rows_ref[8:1080, :].astype(BF16)


def convolve(chan, place, toep_ref, win_ref, conv_ref):
    sums = ([None] * 8, [None] * 8)
    for cols in range(4):
        window = jnp.concatenate(
            [win_ref[16 * deep + 256 * cols:16 * deep + 256 * (cols + 1), :] for deep in range(DEPTH // 256)], axis=1
        )
        part = dot_nt(toep_ref[chan, 64 * cols:256, :], window)
        for lag in range(16 - 4 * cols):
            row = TAP * (15 - lag - 4 * cols)
            for side in range(2):
                tile = 2 * cols + side + lag // 2
                if tile < 8:
                    piece = part[row:row + TAP, 128 * side:128 * (side + 1)]
                    old = sums[lag % 2][tile]
                    sums[lag % 2][tile] = piece if old is None else old + piece
    first_half = iota((TAP, 128), 1) < 64
    earlier = jnp.zeros((TAP, 128), F32)
    for tile in range(8):
        turned = pltpu.roll(sums[1][tile], 64, 1)
        conv_ref[tile, pl.ds(pl.multiple_of(place * TAP, TAP), TAP), :] = sums[0][tile] + jnp.where(
            first_half, earlier, turned
        )
        earlier = turned


def block_kernel(sig_ref, gate_ref, skip_ref, decay_ref, w1_ref, b1_ref, w2_ref, b2_ref, hi_ref, fix_ref, wout_ref,
                 out_ref,
                 first_ref, second_ref, bias_ref, third_ref, env_ref, filt_ref, toep_ref, rows_ref, win_ref, conv_ref,
                 send_x, recv_x, turn_ref, send_y0, send_y1, send_y2, recv_y0, recv_y1, recv_y2, gated_ref, wide_ref, total_ref, mixed_ref,
                 core_send, core_recv, far_send, far_recv,
                 wide_sem, x_send_sem, x_recv_sem, y_send_sem, y_recv_sem,
                 core_send_sem, core_recv_sem, far_send_sem, far_recv_sem, out_sem):
    me = lax.axis_index("seq")
    group = lax.axis_index("ch")
    core = lax.rem(group, 2)
    chip = lax.div(group, 2)
    core_mate = chip * 2 + 1 - core
    far_mate = (1 - chip) * 2 + core

    barrier = pltpu.get_barrier_semaphore()

    @pl.loop(1, DEVS)
    def _(step):
        pl.semaphore_signal(barrier, inc=1, device_id={"seq": lax.rem(me + step, DEVS)}, device_id_type=MESH)

    for mate in (core_mate, far_mate):
        pl.semaphore_signal(barrier, inc=1, device_id={"ch": mate}, device_id_type=MESH)

    blocks = ((1 - chip) * 2 + 1 - core, far_mate, core_mate, group)
    loads = [
        pltpu.make_async_copy(
            wout_ref.at[:, pl.ds(pl.multiple_of(block * COLS, COLS), COLS)], wide_ref.at[slot], wide_sem.at[slot]
        )
        for slot, block in enumerate(blocks)
    ]
    for load in loads:
        load.start()

    for half in range(2):
        turned = sig_ref[128 * half:128 * (half + 1), :].astype(F32).T
        for chan in range(OWN):
            send_x[chan // SUB, pl.ds(SUB * half + chan % SUB, DEVS, stride=8), :] = (
                turned[DEVS * chan:DEVS * (chan + 1), :]
            )
    own_send = pl.ds(pl.multiple_of(me * 8, 8), 8)
    own_recv = pl.ds(pl.multiple_of(me * 8 + 8, 8), 8)
    for group_num in range(2):
        recv_x[group_num, 0:8, :] = jnp.zeros((8, 128), F32)
        recv_x[group_num, own_recv, :] = send_x[group_num, own_send, :]
    filter_weights(me, decay_ref, w1_ref, b1_ref, w2_ref, b2_ref, hi_ref, fix_ref,
                   first_ref, second_ref, bias_ref, third_ref, env_ref)
    pl.semaphore_wait(barrier, DEVS + 1)

    for group_num in range(2):

        @pl.loop(1, DEVS)
        def _(step):
            peer = lax.rem(me + step, DEVS)
            pltpu.make_async_remote_copy(
                src_ref=send_x.at[group_num, pl.ds(pl.multiple_of(peer * 8, 8), 8), :],
                dst_ref=recv_x.at[group_num, own_recv, :],
                send_sem=x_send_sem.at[group_num],
                recv_sem=x_recv_sem.at[group_num],
                device_id={"seq": peer},
                device_id_type=MESH,
            ).start()

    @pl.loop(0, QUARTER // STEP)
    def _(step):
        filter_step(step, first_ref, second_ref, bias_ref, third_ref, env_ref, filt_ref)

    toeplitz_tiles(filt_ref, toep_ref)

    rows_ref[0:56, :] = jnp.zeros((56, 128), F32)
    pieces = ((0, 0, 8), (1, 0, 2), (1, 2, 6))
    outgoing, incoming = (send_y0, send_y1, send_y2), (recv_y0, recv_y1, recv_y2)

    def own_piece(size):
        return pl.ds(pl.multiple_of(me * size, 2), size)

    def return_rows(group_num):
        even_half = iota((64, 128), 1) < 64
        for tile in range(8):
            value = conv_ref[group_num, tile]
            turn_ref[tile] = jnp.concatenate([value, value], axis=0).T
            block = jnp.where(
                even_half, turn_ref[tile, pl.ds(0, 64, stride=2), :], turn_ref[tile, pl.ds(1, 64, stride=2), :]
            )
            for slot, (which, first, size) in enumerate(pieces):
                if which == group_num:
                    if size == 8:
                        outgoing[slot][64 * tile:64 * (tile + 1), :] = block
                    else:
                        for peer in range(8):
                            place = (8 * tile + peer) * size
                            row = 8 * peer + first
                            outgoing[slot][place:place + size, :] = block[row:row + size, :]
        for slot, (which, _, size) in enumerate(pieces):
            if which == group_num:
                incoming[slot][own_piece(size), :] = outgoing[slot][own_piece(size), :]

                @pl.loop(1, DEVS)
                def _(step):
                    peer = lax.rem(me + step, DEVS)
                    pltpu.make_async_remote_copy(
                        src_ref=outgoing[slot].at[pl.ds(pl.multiple_of(peer * size, 2), size), :],
                        dst_ref=incoming[slot].at[own_piece(size), :],
                        send_sem=y_send_sem.at[slot],
                        recv_sem=y_recv_sem.at[slot],
                        device_id={"seq": peer},
                        device_id_type=MESH,
                    ).start()

    def all_pieces(buffers, slot, sems):
        rows = pl.ds(0, (DEVS - 1) * pieces[slot][2])
        return pltpu.make_async_copy(buffers[slot].at[rows, :], buffers[slot].at[rows, :], sems.at[slot])

    many = pl.ds(0, (DEVS - 1) * 8)
    for group_num in range(2):
        pltpu.make_async_copy(
            recv_x.at[group_num, many, :], recv_x.at[group_num, many, :], x_recv_sem.at[group_num]
        ).wait()

        @pl.loop(0, SUB, unroll=2)
        def _(chan):
            signal_windows(chan, recv_x.at[group_num], rows_ref, win_ref)
            convolve(group_num * SUB + chan, chan, toep_ref, win_ref, conv_ref.at[group_num])

        return_rows(group_num)

    def to_core(quarter, which):
        return pltpu.make_async_remote_copy(
            src_ref=core_send.at[quarter, which], dst_ref=core_recv.at[quarter, which],
            send_sem=core_send_sem.at[quarter, which], recv_sem=core_recv_sem.at[quarter, which],
            device_id={"ch": core_mate}, device_id_type=MESH,
        )

    def to_far(quarter):
        return pltpu.make_async_remote_copy(
            src_ref=far_send.at[quarter], dst_ref=far_recv.at[quarter],
            send_sem=far_send_sem.at[quarter], recv_sem=far_recv_sem.at[quarter],
            device_id={"ch": far_mate}, device_id_type=MESH,
        )

    def to_out(quarter):
        return pltpu.make_async_copy(
            mixed_ref.at[quarter], out_ref.at[64 * quarter:64 * (quarter + 1), :], out_sem.at[quarter]
        )

    for load in loads:
        load.wait()
    first_half = iota((16, 128), 1) < 64
    for quarter in range(4):
        if quarter == 0:
            all_pieces(incoming, 0, y_recv_sem).wait()
        if quarter < 2:
            all_pieces(incoming, quarter + 1, y_recv_sem).wait()
        for row in range(2):
            if quarter == 0:
                late = recv_y1[pl.ds(row, DEVS, stride=2), :]
            else:
                late = recv_y2[pl.ds(2 * (quarter - 1) + row, DEVS, stride=6), :]
            both = jnp.concatenate([recv_y0[pl.ds(2 * quarter + row, DEVS, stride=8), :], late], axis=0).T
            swapped = pltpu.roll(both, 64, 1)
            for odd in range(2):
                place = 16 * (2 * row + odd)
                rows = slice(64 * quarter + place, 64 * quarter + place + 16)
                for two in range(OWN // 2):
                    left = 64 * odd + 32 * (two % 2)
                    low, high = slice(left, left + 16), slice(left + 16, left + 32)
                    lanes = slice(128 * two, 128 * (two + 1))
                    if two < 2:
                        value = jnp.where(first_half, both[low], swapped[high])
                    else:
                        value = jnp.where(first_half, swapped[low], both[high])
                    gated_ref[place:place + 16, lanes] = (
                        gate_ref[rows, lanes].astype(F32)
                        * (value + skip_ref[:, lanes] * sig_ref[rows, lanes].astype(F32))
                    ).astype(BF16)
        core_send[quarter, 0] = dot(gated_ref[...], wide_ref[0])
        to_core(quarter, 0).start()
        far_send[quarter] = dot(gated_ref[...], wide_ref[1])
        to_core(quarter, 0).wait_recv()
        far_send[quarter] += core_recv[quarter, 0]
        to_far(quarter).start()
        core_send[quarter, 1] = dot(gated_ref[...], wide_ref[2])
        to_core(quarter, 1).start()
        total_ref[quarter] = dot(gated_ref[...], wide_ref[3])
    for quarter in range(4):
        to_core(quarter, 1).wait_recv()
        to_far(quarter).wait_recv()
        mixed_ref[quarter] = (total_ref[quarter] + core_recv[quarter, 1] + far_recv[quarter]).astype(BF16)
        to_out(quarter).start()
    for quarter in range(4):
        to_out(quarter).wait()

    for group_num in range(2):
        pltpu.make_async_copy(
            send_x.at[group_num, many, :], send_x.at[group_num, many, :], x_send_sem.at[group_num]
        ).wait()
    for slot in range(3):
        all_pieces(outgoing, slot, y_send_sem).wait()
    for quarter in range(4):
        for which in range(2):
            to_core(quarter, which).wait_send()
        to_far(quarter).wait_send()


def shards(signal, gate_in, skip_gain, decay, pos_weight1, pos_bias1, pos_weight2, pos_bias2, filt_hi, filt_fix,
           out_weight):
    vmem = pl.BlockSpec(memory_space=pltpu.VMEM)
    wide = PARTS * HID
    return pl.pallas_call(
        block_kernel,
        out_shape=jax.ShapeDtypeStruct((ROWS, COLS), BF16),
        in_specs=[vmem] * 10 + [pl.BlockSpec(memory_space=pl.ANY)],
        out_specs=pl.BlockSpec(memory_space=pl.ANY),
        scratch_shapes=[
            pltpu.VMEM((128, wide), BF16),
            pltpu.VMEM((2, wide, wide), BF16),
            pltpu.VMEM((1, wide), F32),
            pltpu.VMEM((2 * PARTS * OWN, wide), BF16),
            pltpu.VMEM((PARTS * OWN, 128), F32),
            pltpu.VMEM((QUARTER // 128, PARTS * OWN, 128), F32),
            pltpu.VMEM((OWN, SEQ_LEN // DEPTH * TAP, DEPTH), BF16),
            pltpu.VMEM((1088, 128), F32),
            pltpu.VMEM((1072, 256), BF16),
            pltpu.VMEM((2, 8, SUB * TAP, 128), F32),
            pltpu.VMEM((2, DEVS * 8, 128), F32),
            pltpu.VMEM((2, DEVS * 8 + 8, 128), F32),
            pltpu.VMEM((8, 128, 128), F32),
            pltpu.VMEM((DEVS * 8, 128), F32),
            pltpu.VMEM((DEVS * 2, 128), F32),
            pltpu.VMEM((DEVS * 6, 128), F32),
            pltpu.VMEM((DEVS * 8, 128), F32),
            pltpu.VMEM((DEVS * 2, 128), F32),
            pltpu.VMEM((DEVS * 6, 128), F32),
            pltpu.VMEM((64, CHANS), BF16),
            pltpu.VMEM((4, CHANS, COLS), BF16),
            pltpu.VMEM((4, 64, COLS), F32),
            pltpu.VMEM((4, 64, COLS), BF16),
            pltpu.VMEM((4, 2, 64, COLS), F32),
            pltpu.VMEM((4, 2, 64, COLS), F32),
            pltpu.VMEM((4, 64, COLS), F32),
            pltpu.VMEM((4, 64, COLS), F32),
            pltpu.SemaphoreType.DMA((4,)),
            pltpu.SemaphoreType.DMA((2,)),
            pltpu.SemaphoreType.DMA((2,)),
            pltpu.SemaphoreType.DMA((4,)),
            pltpu.SemaphoreType.DMA((4,)),
            pltpu.SemaphoreType.DMA((4, 2)),
            pltpu.SemaphoreType.DMA((4, 2)),
            pltpu.SemaphoreType.DMA((4,)),
            pltpu.SemaphoreType.DMA((4,)),
            pltpu.SemaphoreType.DMA((4,)),
        ],
        compiler_params=pltpu.CompilerParams(
            collective_id=0, has_side_effects=True, vmem_limit_bytes=56 * 2**20
        ),
        name="hyena_block",
    )(
        signal, gate_in, skip_gain[None, :], decay[None, :], pos_weight1, pos_bias1[None, :], pos_weight2,
        pos_bias2[None, :], filt_hi, filt_fix, out_weight,
    )


def solution(mesh):
    return jax.shard_map(
        shards,
        mesh=mesh,
        in_specs=(
            P("seq", "ch"), P("seq", "ch"), P("ch"), P("ch"), P(), P(), P(), P(), P(None, "ch"), P(None, "ch"),
            P("ch", None),
        ),
        out_specs=P("seq", "ch"),
        check_vma=False,
    )
```

```python
import math

import jax
import jax.numpy as jnp
from jax import lax
from jax.experimental import pallas as pl
from jax.experimental.pallas import tpu as pltpu
from jax.sharding import PartitionSpec as P

F32 = jnp.float32
BF16 = jnp.bfloat16
MESH = pl.DeviceIdType.MESH

SEQ_LEN = 16384
DEVS = 64
ROWS = 256
CHANS = 512
OWN = 8
SUB = 4
GROUPS = ((0, 4), (4, 2), (6, 2))
HID = 64
PARTS = 4
QUARTER = SEQ_LEN // PARTS
STEP = 1024
TAP = 16
DEPTH = 1024
DEPTH_PER_PART = QUARTER // DEPTH
TOP = SEQ_LEN - TAP
COLS = 1024
INV_TURN = 1.0 / (2.0 * math.pi)
COS_POLY = (6.283185159611168, -41.34165492934356, 81.60099819261757, -76.54965682073457, 39.53581371237487)


def turn_cos(turns):
    near = turns - jnp.round(turns)
    arg = 0.25 - jnp.abs(near)
    square = arg * arg
    c0, c1, c2, c3, c4 = COS_POLY
    return arg * (c0 + square * (c1 + square * (c2 + square * (c3 + square * c4))))


def split_two(value):
    high = value.astype(BF16)
    return high, (value - high.astype(F32)).astype(BF16)


def dot(left, right):
    return jnp.dot(left, right, preferred_element_type=F32)


def dot_nt(left, right):
    return lax.dot_general(left, right, (((1,), (1,)), ((), ())), preferred_element_type=F32)


def tile_lanes(value):
    return jnp.concatenate([value] * PARTS, axis=1)


def iota(shape, axis):
    return lax.broadcasted_iota(jnp.int32, shape, axis)


def filter_weights(own_first, decay_ref, w1_ref, b1_ref, w2_ref, b2_ref, hi_ref, fix_ref,
                   first_ref, second_ref, bias_ref, third_ref, env_ref):
    wide = PARTS * HID
    part = iota((16, wide), 1) >> 6
    freq = (iota((16, wide), 0) + 1).astype(F32)
    turns = freq * (TOP - QUARTER * part).astype(F32) * (1.0 / SEQ_LEN)
    cos_top, sin_top = turn_cos(turns), turn_cos(turns - 0.25)
    w_lin = tile_lanes(w1_ref[0:1, :]) * INV_TURN
    w_cos = tile_lanes(w1_ref[1:17, :]) * INV_TURN
    w_sin = tile_lanes(w1_ref[17:33, :]) * INV_TURN
    main = jnp.concatenate(
        [w_cos * cos_top + w_sin * sin_top, w_cos * sin_top - w_sin * cos_top], axis=0
    )
    main_hi = main.astype(BF16).astype(F32)
    main_lo = main - main_hi
    part_row = iota((1, wide), 1) >> 6
    top_row = (TOP - QUARTER * part_row).astype(F32) * (1.0 / SEQ_LEN)
    slope = -w_lin / PARTS
    const = w_lin * top_row + tile_lanes(b1_ref[...]) * INV_TURN - 0.25
    wrap = jnp.where(part_row == PARTS - 1, w_lin, 0.0)
    extra = jnp.zeros((32, wide), F32)
    row = iota((32, wide), 0)
    place = 0
    for value, pieces, repeat in ((slope, 2, 2), (const, 3, 1), (wrap, 3, 1)):
        rest = value
        for _ in range(pieces):
            piece = rest.astype(BF16).astype(F32)
            rest = rest - piece
            for _ in range(repeat):
                extra = jnp.where(row == place, piece, extra)
                place += 1
    first_ref[...] = jnp.concatenate([main_hi, main_hi, main_lo, extra], axis=0).astype(BF16)

    own_block = iota((wide, wide), 0) >> 6 == iota((wide, wide), 1) >> 6
    w2_rows = jnp.concatenate([w2_ref[...] * INV_TURN] * PARTS, axis=0)
    w2_full = jnp.where(own_block, tile_lanes(w2_rows), 0.0)
    w2_hi, w2_lo = split_two(w2_full)
    second_ref[0] = w2_hi
    second_ref[1] = w2_lo
    bias_ref[...] = tile_lanes(b2_ref[...]) * INV_TURN - 0.25

    lhs_rows = PARTS * OWN
    pick = iota((lhs_rows, CHANS), 1) == own_first + DEVS * (iota((lhs_rows, CHANS), 0) & (OWN - 1))
    chosen = jnp.where(pick, 1.0, 0.0).astype(BF16)
    keep = iota((lhs_rows, wide), 1) >> 6 == iota((lhs_rows, wide), 0) >> 3
    hi_part = jnp.concatenate([hi_ref[...]] * PARTS, axis=0)
    fix_part = jnp.concatenate([(fix_ref[...].astype(F32) * 2.0 ** (-11)).astype(BF16)] * PARTS, axis=0)
    third_ref[...] = jnp.concatenate(
        [jnp.where(keep, dot_nt(chosen, hi_part), 0.0), jnp.where(keep, dot_nt(chosen, fix_part), 0.0)], axis=0
    ).astype(BF16)
    env_ref[...] = jnp.broadcast_to(
        jnp.sum(jnp.where(pick, decay_ref[...], 0.0), axis=1, keepdims=True), (lhs_rows, 128)
    )


def filter_step(step, first_ref, second_ref, bias_ref, third_ref, env_ref, filt_ref):
    lane = iota((1, 128), 1)
    where_in = (iota((STEP, 128), 0) + step * STEP).astype(F32)
    rate = ((lane & 15) + 1).astype(F32) * (1.0 / SEQ_LEN)
    shift = jnp.where((lane & 16) == 0, 0.0, 0.25)
    slope = jnp.where(lane < 100, 1.0 / QUARTER, 0.0)
    start = jnp.where((lane >= 100) & (lane < 103), 1.0, 0.0)
    turn = jnp.where((lane >= 103) & (lane < 106), float(TOP - QUARTER * (PARTS - 1)), float(SEQ_LEN))
    value = jnp.where(lane < 96, turn_cos(where_in * rate - shift), where_in * slope + start)
    value = jnp.where(where_in > turn, 1.0, value)
    low = ((lane >= 32) & (lane < 64)) | (lane == 97) | (lane == 99)
    high = value.astype(BF16).astype(F32)
    feats = jnp.where(low, value - high, high).astype(BF16)
    one_hi, one_lo = split_two(turn_cos(dot(feats, first_ref[...])))
    turns = dot(one_hi, second_ref[0]) + dot(one_lo, second_ref[0]) + dot(one_hi, second_ref[1])
    two_hi, two_lo = split_two(turn_cos(turns + bias_ref[...]))
    both = dot_nt(third_ref[...], two_hi) + dot_nt(third_ref[...], two_lo)
    lhs_rows = PARTS * OWN
    shape = (lhs_rows, STEP)
    time = TOP - QUARTER * ((iota(shape, 0) >> 3)) - (iota(shape, 1) + step * STEP)
    time = jnp.where(time < 0, time + SEQ_LEN, time).astype(F32)
    rate = jnp.concatenate([env_ref[...]] * (STEP // 128), axis=1)
    envelope = jnp.exp(-rate * time) * jnp.sqrt(2.0 * rate + 1.0 / SEQ_LEN)
    filters = (both[:lhs_rows] + both[lhs_rows:]) * envelope
    for tile in range(STEP // 128):
        filt_ref[step * (STEP // 128) + tile] = filters[:, 128 * tile:128 * (tile + 1)]


def toeplitz_tiles(filt_ref, toep_ref):
    shape = (TAP, 128)
    ahead = iota(shape, 1) >= iota(shape, 0)
    inside = iota(shape, 1) <= iota(shape, 0) + (128 - TAP)
    per_part = QUARTER // 128

    def slanted(part, tile):
        taps = filt_ref[tile, pl.ds(pl.multiple_of(part * OWN, OWN), OWN), :]
        return tuple(
            pltpu.roll(jnp.broadcast_to(taps[chan:chan + 1], shape), 0, 1, stride=1, stride_axis=0)
            for chan in range(OWN)
        )

    def block(index, before):
        part = lax.div(index, DEPTH_PER_PART)
        first = lax.rem(index, DEPTH_PER_PART) * (DEPTH // 128)
        for sub in range(DEPTH // 128):
            now = slanted(part, first + sub)
            for chan in range(OWN):
                tile = jnp.where(ahead, now[chan], before[chan])
                if sub == DEPTH // 128 - 1:
                    tile = jnp.where(inside | (index < SEQ_LEN // DEPTH - 1), tile, 0.0)
                toep_ref[chan, pl.ds(pl.multiple_of(index * TAP, TAP), TAP), sub * 128:(sub + 1) * 128] = tile.astype(BF16)
            before = now
        return before

    lax.fori_loop(0, SEQ_LEN // DEPTH, block, slanted(PARTS - 1, per_part - 1))


def signal_windows(chan, count, recv_ref, rows_ref, win_ref):
    lane = iota((128, 128), 1)
    before = recv_ref[pl.ds(8 - count + chan, 128, stride=count), :]
    after = recv_ref[pl.ds(8 + chan, 128, stride=count), :]
    for sub in range(8):
        ahead = TAP * (sub + 1)
        value = after
        if ahead < 128:
            value = pltpu.roll(jnp.where(lane >= ahead, before, after), 128 - ahead, 1)
        rows_ref[pl.ds(56 + sub, 128, stride=8), :] = value
    win_ref[:, 0:128] = rows_ref[0:1072, :].astype(BF16)
    win_ref[:, 128:256] = rows_ref[8:1080, :].astype(BF16)


def convolve(chan, place, toep_ref, win_ref, conv_ref):
    sums = ([None] * 8, [None] * 8)
    for cols in range(4):
        window = jnp.concatenate(
            [win_ref[16 * deep + 256 * cols:16 * deep + 256 * (cols + 1), :] for deep in range(DEPTH // 256)], axis=1
        )
        part = dot_nt(toep_ref[chan, 64 * cols:256, :], window)
        for lag in range(16 - 4 * cols):
            row = TAP * (15 - lag - 4 * cols)
            for side in range(2):
                tile = 2 * cols + side + lag // 2
                if tile < 8:
                    piece = part[row:row + TAP, 128 * side:128 * (side + 1)]
                    old = sums[lag % 2][tile]
                    sums[lag % 2][tile] = piece if old is None else old + piece
    first_half = iota((TAP, 128), 1) < 64
    earlier = jnp.zeros((TAP, 128), F32)
    for tile in range(8):
        turned = pltpu.roll(sums[1][tile], 64, 1)
        conv_ref[tile, pl.ds(pl.multiple_of(place * TAP, TAP), TAP), :] = sums[0][tile] + jnp.where(
            first_half, earlier, turned
        )
        earlier = turned


def block_kernel(sig_ref, gate_ref, skip_ref, decay_ref, w1_ref, b1_ref, w2_ref, b2_ref, hi_ref, fix_ref, wout_ref,
                 out_ref,
                 first_ref, second_ref, bias_ref, third_ref, env_ref, filt_ref, toep_ref, rows_ref, win_ref, conv_ref,
                 send_x0, send_x1, send_x2, recv_x0, recv_x1, recv_x2, turn_ref, send_y0, send_y1, send_y2, recv_y0, recv_y1, recv_y2, gated_ref, wide_ref, total_ref, mixed_ref,
                 core_send, core_recv, far_send, far_recv,
                 wide_sem, x_send_sem, x_recv_sem, y_send_sem, y_recv_sem,
                 core_send_sem, core_recv_sem, far_send_sem, far_recv_sem, out_sem):
    me = lax.axis_index("seq")
    group = lax.axis_index("ch")
    core = lax.rem(group, 2)
    chip = lax.div(group, 2)
    core_mate = chip * 2 + 1 - core
    far_mate = (1 - chip) * 2 + core

    barrier = pltpu.get_barrier_semaphore()

    @pl.loop(1, DEVS)
    def _(step):
        pl.semaphore_signal(barrier, inc=1, device_id={"seq": lax.rem(me + step, DEVS)}, device_id_type=MESH)

    for mate in (core_mate, far_mate):
        pl.semaphore_signal(barrier, inc=1, device_id={"ch": mate}, device_id_type=MESH)

    blocks = ((1 - chip) * 2 + 1 - core, far_mate, core_mate, group)
    loads = [
        pltpu.make_async_copy(
            wout_ref.at[:, pl.ds(pl.multiple_of(block * COLS, COLS), COLS)], wide_ref.at[slot], wide_sem.at[slot]
        )
        for slot, block in enumerate(blocks)
    ]
    for load in loads:
        load.start()

    leaving, landing = (send_x0, send_x1, send_x2), (recv_x0, recv_x1, recv_x2)
    for half in range(2):
        turned = sig_ref[128 * half:128 * (half + 1), :].astype(F32).T
        for slot, (first, count) in enumerate(GROUPS):
            for chan in range(count):
                place = DEVS * (first + chan)
                leaving[slot][pl.ds(count * half + chan, DEVS, stride=2 * count), :] = turned[place:place + DEVS, :]

    def block_rows(device, count, offset=0):
        return pl.ds(pl.multiple_of(device * (2 * count) + offset, 4), 2 * count)

    for slot, (_, count) in enumerate(GROUPS):
        landing[slot][0:8, :] = jnp.zeros((8, 128), F32)
        landing[slot][block_rows(me, count, 8), :] = leaving[slot][block_rows(me, count), :]
    filter_weights(me, decay_ref, w1_ref, b1_ref, w2_ref, b2_ref, hi_ref, fix_ref,
                   first_ref, second_ref, bias_ref, third_ref, env_ref)
    pl.semaphore_wait(barrier, DEVS + 1)

    for slot, (_, count) in enumerate(GROUPS):

        @pl.loop(1, DEVS)
        def _(step):
            peer = lax.rem(me + step, DEVS)
            pltpu.make_async_remote_copy(
                src_ref=leaving[slot].at[block_rows(peer, count), :],
                dst_ref=landing[slot].at[block_rows(me, count, 8), :],
                send_sem=x_send_sem.at[slot],
                recv_sem=x_recv_sem.at[slot],
                device_id={"seq": peer},
                device_id_type=MESH,
            ).start()

    @pl.loop(0, QUARTER // STEP)
    def _(step):
        filter_step(step, first_ref, second_ref, bias_ref, third_ref, env_ref, filt_ref)

    toeplitz_tiles(filt_ref, toep_ref)

    rows_ref[0:56, :] = jnp.zeros((56, 128), F32)
    pieces = ((0, 0, 8), (1, 0, 2), (1, 2, 6))
    outgoing, incoming = (send_y0, send_y1, send_y2), (recv_y0, recv_y1, recv_y2)

    def own_piece(size):
        return pl.ds(pl.multiple_of(me * size, 2), size)

    def return_rows(group_num):
        even_half = iota((64, 128), 1) < 64
        for tile in range(8):
            value = conv_ref[group_num, tile]
            turn_ref[tile] = jnp.concatenate([value, value], axis=0).T
            block = jnp.where(
                even_half, turn_ref[tile, pl.ds(0, 64, stride=2), :], turn_ref[tile, pl.ds(1, 64, stride=2), :]
            )
            for slot, (which, first, size) in enumerate(pieces):
                if which == group_num:
                    if size == 8:
                        outgoing[slot][64 * tile:64 * (tile + 1), :] = block
                    else:
                        for peer in range(8):
                            place = (8 * tile + peer) * size
                            row = 8 * peer + first
                            outgoing[slot][place:place + size, :] = block[row:row + size, :]
        for slot, (which, _, size) in enumerate(pieces):
            if which == group_num:
                incoming[slot][own_piece(size), :] = outgoing[slot][own_piece(size), :]

                def send_piece(peer):
                    pltpu.make_async_remote_copy(
                        src_ref=outgoing[slot].at[pl.ds(pl.multiple_of(peer * size, 2), size), :],
                        dst_ref=incoming[slot].at[own_piece(size), :],
                        send_sem=y_send_sem.at[slot],
                        recv_sem=y_recv_sem.at[slot],
                        device_id={"seq": peer},
                        device_id_type=MESH,
                    ).start()

                x_half = lax.div(me, DEVS // 2)

                @pl.loop(0, DEVS // 2)
                def _(step):
                    send_piece((1 - x_half) * (DEVS // 2) + lax.rem(me + step, DEVS // 2))

                @pl.loop(1, DEVS // 2)
                def _(step):
                    send_piece(x_half * (DEVS // 2) + lax.rem(me + step, DEVS // 2))

    def all_pieces(buffers, slot, sems):
        rows = pl.ds(0, (DEVS - 1) * pieces[slot][2])
        return pltpu.make_async_copy(buffers[slot].at[rows, :], buffers[slot].at[rows, :], sems.at[slot])

    def all_blocks(buffers, slot, sems):
        rows = pl.ds(0, (DEVS - 1) * 2 * GROUPS[slot][1])
        return pltpu.make_async_copy(buffers[slot].at[rows, :], buffers[slot].at[rows, :], sems.at[slot])

    for slot, (first, count) in enumerate(GROUPS):
        all_blocks(landing, slot, x_recv_sem).wait()

        @pl.loop(0, count, unroll=2)
        def _(chan):
            signal_windows(chan, count, landing[slot], rows_ref, win_ref)
            convolve(first + chan, first % SUB + chan, toep_ref, win_ref, conv_ref.at[first // SUB])

        if (first + count) % SUB == 0:
            return_rows(first // SUB)

    def to_core(quarter, which):
        return pltpu.make_async_remote_copy(
            src_ref=core_send.at[quarter, which], dst_ref=core_recv.at[quarter, which],
            send_sem=core_send_sem.at[quarter, which], recv_sem=core_recv_sem.at[quarter, which],
            device_id={"ch": core_mate}, device_id_type=MESH,
        )

    def to_far(quarter):
        return pltpu.make_async_remote_copy(
            src_ref=far_send.at[quarter], dst_ref=far_recv.at[quarter],
            send_sem=far_send_sem.at[quarter], recv_sem=far_recv_sem.at[quarter],
            device_id={"ch": far_mate}, device_id_type=MESH,
        )

    def to_out(quarter):
        return pltpu.make_async_copy(
            mixed_ref.at[quarter], out_ref.at[64 * quarter:64 * (quarter + 1), :], out_sem.at[quarter]
        )

    for load in loads:
        load.wait()
    first_half = iota((16, 128), 1) < 64
    for quarter in range(4):
        if quarter == 0:
            all_pieces(incoming, 0, y_recv_sem).wait()
        if quarter < 2:
            all_pieces(incoming, quarter + 1, y_recv_sem).wait()
        for row in range(2):
            if quarter == 0:
                late = recv_y1[pl.ds(row, DEVS, stride=2), :]
            else:
                late = recv_y2[pl.ds(2 * (quarter - 1) + row, DEVS, stride=6), :]
            both = jnp.concatenate([recv_y0[pl.ds(2 * quarter + row, DEVS, stride=8), :], late], axis=0).T
            swapped = pltpu.roll(both, 64, 1)
            for odd in range(2):
                place = 16 * (2 * row + odd)
                rows = slice(64 * quarter + place, 64 * quarter + place + 16)
                for two in range(OWN // 2):
                    left = 64 * odd + 32 * (two % 2)
                    low, high = slice(left, left + 16), slice(left + 16, left + 32)
                    lanes = slice(128 * two, 128 * (two + 1))
                    if two < 2:
                        value = jnp.where(first_half, both[low], swapped[high])
                    else:
                        value = jnp.where(first_half, swapped[low], both[high])
                    gated_ref[place:place + 16, lanes] = (
                        gate_ref[rows, lanes].astype(F32)
                        * (value + skip_ref[:, lanes] * sig_ref[rows, lanes].astype(F32))
                    ).astype(BF16)
        core_send[quarter, 0] = dot(gated_ref[...], wide_ref[0])
        to_core(quarter, 0).start()
        far_send[quarter] = dot(gated_ref[...], wide_ref[1])
        to_core(quarter, 0).wait_recv()
        far_send[quarter] += core_recv[quarter, 0]
        to_far(quarter).start()
        core_send[quarter, 1] = dot(gated_ref[...], wide_ref[2])
        to_core(quarter, 1).start()
        total_ref[quarter] = dot(gated_ref[...], wide_ref[3])
    for quarter in range(4):
        to_core(quarter, 1).wait_recv()
        to_far(quarter).wait_recv()
        mixed_ref[quarter] = (total_ref[quarter] + core_recv[quarter, 1] + far_recv[quarter]).astype(BF16)
        to_out(quarter).start()
    for quarter in range(4):
        to_out(quarter).wait()

    for slot in range(3):
        all_blocks(leaving, slot, x_send_sem).wait()
    for slot in range(3):
        all_pieces(outgoing, slot, y_send_sem).wait()
    for quarter in range(4):
        for which in range(2):
            to_core(quarter, which).wait_send()
        to_far(quarter).wait_send()


def shards(signal, gate_in, skip_gain, decay, pos_weight1, pos_bias1, pos_weight2, pos_bias2, filt_hi, filt_fix,
           out_weight):
    vmem = pl.BlockSpec(memory_space=pltpu.VMEM)
    wide = PARTS * HID
    return pl.pallas_call(
        block_kernel,
        out_shape=jax.ShapeDtypeStruct((ROWS, COLS), BF16),
        in_specs=[vmem] * 10 + [pl.BlockSpec(memory_space=pl.ANY)],
        out_specs=pl.BlockSpec(memory_space=pl.ANY),
        scratch_shapes=[
            pltpu.VMEM((128, wide), BF16),
            pltpu.VMEM((2, wide, wide), BF16),
            pltpu.VMEM((1, wide), F32),
            pltpu.VMEM((2 * PARTS * OWN, wide), BF16),
            pltpu.VMEM((PARTS * OWN, 128), F32),
            pltpu.VMEM((QUARTER // 128, PARTS * OWN, 128), F32),
            pltpu.VMEM((OWN, SEQ_LEN // DEPTH * TAP, DEPTH), BF16),
            pltpu.VMEM((1088, 128), F32),
            pltpu.VMEM((1072, 256), BF16),
            pltpu.VMEM((2, 8, SUB * TAP, 128), F32),
            pltpu.VMEM((DEVS * 8, 128), F32),
            pltpu.VMEM((DEVS * 4, 128), F32),
            pltpu.VMEM((DEVS * 4, 128), F32),
            pltpu.VMEM((DEVS * 8 + 8, 128), F32),
            pltpu.VMEM((DEVS * 4 + 8, 128), F32),
            pltpu.VMEM((DEVS * 4 + 8, 128), F32),
            pltpu.VMEM((8, 128, 128), F32),
            pltpu.VMEM((DEVS * 8, 128), F32),
            pltpu.VMEM((DEVS * 2, 128), F32),
            pltpu.VMEM((DEVS * 6, 128), F32),
            pltpu.VMEM((DEVS * 8, 128), F32),
            pltpu.VMEM((DEVS * 2, 128), F32),
            pltpu.VMEM((DEVS * 6, 128), F32),
            pltpu.VMEM((64, CHANS), BF16),
            pltpu.VMEM((4, CHANS, COLS), BF16),
            pltpu.VMEM((4, 64, COLS), F32),
            pltpu.VMEM((4, 64, COLS), BF16),
            pltpu.VMEM((4, 2, 64, COLS), F32),
            pltpu.VMEM((4, 2, 64, COLS), F32),
            pltpu.VMEM((4, 64, COLS), F32),
            pltpu.VMEM((4, 64, COLS), F32),
            pltpu.SemaphoreType.DMA((4,)),
            pltpu.SemaphoreType.DMA((3,)),
            pltpu.SemaphoreType.DMA((3,)),
            pltpu.SemaphoreType.DMA((4,)),
            pltpu.SemaphoreType.DMA((4,)),
            pltpu.SemaphoreType.DMA((4, 2)),
            pltpu.SemaphoreType.DMA((4, 2)),
            pltpu.SemaphoreType.DMA((4,)),
            pltpu.SemaphoreType.DMA((4,)),
            pltpu.SemaphoreType.DMA((4,)),
        ],
        compiler_params=pltpu.CompilerParams(
            collective_id=0, has_side_effects=True, vmem_limit_bytes=56 * 2**20
        ),
        name="hyena_block",
    )(
        signal, gate_in, skip_gain[None, :], decay[None, :], pos_weight1, pos_bias1[None, :], pos_weight2,
        pos_bias2[None, :], filt_hi, filt_fix, out_weight,
    )


def solution(mesh):
    return jax.shard_map(
        shards,
        mesh=mesh,
        in_specs=(
            P("seq", "ch"), P("seq", "ch"), P("ch"), P("ch"), P(), P(), P(), P(), P(None, "ch"), P(None, "ch"),
            P("ch", None),
        ),
        out_specs=P("seq", "ch"),
        check_vma=False,
    )
```

```python
import math

import jax
import jax.numpy as jnp
from jax import lax
from jax.experimental import pallas as pl
from jax.experimental.pallas import tpu as pltpu
from jax.sharding import PartitionSpec as P

F32 = jnp.float32
BF16 = jnp.bfloat16
MESH = pl.DeviceIdType.MESH

SEQ_LEN = 16384
DEVS = 64
ROWS = 256
CHANS = 512
OWN = 8
SUB = 4
HID = 64
PARTS = 4
QUARTER = SEQ_LEN // PARTS
STEP = 1024
TAP = 16
DEPTH = 1024
DEPTH_PER_PART = QUARTER // DEPTH
TOP = SEQ_LEN - TAP
COLS = 1024
INV_TURN = 1.0 / (2.0 * math.pi)
COS_POLY = (6.283185159611168, -41.34165492934356, 81.60099819261757, -76.54965682073457, 39.53581371237487)


def turn_cos(turns):
    near = turns - jnp.round(turns)
    arg = 0.25 - jnp.abs(near)
    square = arg * arg
    c0, c1, c2, c3, c4 = COS_POLY
    return arg * (c0 + square * (c1 + square * (c2 + square * (c3 + square * c4))))


def split_two(value):
    high = value.astype(BF16)
    return high, (value - high.astype(F32)).astype(BF16)


def dot(left, right):
    return jnp.dot(left, right, preferred_element_type=F32)


def dot_nt(left, right):
    return lax.dot_general(left, right, (((1,), (1,)), ((), ())), preferred_element_type=F32)


def tile_lanes(value):
    return jnp.concatenate([value] * PARTS, axis=1)


def iota(shape, axis):
    return lax.broadcasted_iota(jnp.int32, shape, axis)


def filter_weights(own_first, decay_ref, w1_ref, b1_ref, w2_ref, b2_ref, hi_ref, fix_ref,
                   first_ref, second_ref, bias_ref, third_ref, env_ref):
    wide = PARTS * HID
    part = iota((16, wide), 1) >> 6
    freq = (iota((16, wide), 0) + 1).astype(F32)
    turns = freq * (TOP - QUARTER * part).astype(F32) * (1.0 / SEQ_LEN)
    cos_top, sin_top = turn_cos(turns), turn_cos(turns - 0.25)
    w_lin = tile_lanes(w1_ref[0:1, :]) * INV_TURN
    w_cos = tile_lanes(w1_ref[1:17, :]) * INV_TURN
    w_sin = tile_lanes(w1_ref[17:33, :]) * INV_TURN
    main = jnp.concatenate(
        [w_cos * cos_top + w_sin * sin_top, w_cos * sin_top - w_sin * cos_top], axis=0
    )
    main_hi = main.astype(BF16).astype(F32)
    main_lo = main - main_hi
    part_row = iota((1, wide), 1) >> 6
    top_row = (TOP - QUARTER * part_row).astype(F32) * (1.0 / SEQ_LEN)
    slope = -w_lin / PARTS
    const = w_lin * top_row + tile_lanes(b1_ref[...]) * INV_TURN - 0.25
    wrap = jnp.where(part_row == PARTS - 1, w_lin, 0.0)
    extra = jnp.zeros((32, wide), F32)
    row = iota((32, wide), 0)
    place = 0
    for value, pieces, repeat in ((slope, 2, 2), (const, 3, 1), (wrap, 3, 1)):
        rest = value
        for _ in range(pieces):
            piece = rest.astype(BF16).astype(F32)
            rest = rest - piece
            for _ in range(repeat):
                extra = jnp.where(row == place, piece, extra)
                place += 1
    first_ref[...] = jnp.concatenate([main_hi, main_hi, main_lo, extra], axis=0).astype(BF16)

    own_block = iota((wide, wide), 0) >> 6 == iota((wide, wide), 1) >> 6
    w2_rows = jnp.concatenate([w2_ref[...] * INV_TURN] * PARTS, axis=0)
    w2_full = jnp.where(own_block, tile_lanes(w2_rows), 0.0)
    w2_hi, w2_lo = split_two(w2_full)
    second_ref[0] = w2_hi
    second_ref[1] = w2_lo
    bias_ref[...] = tile_lanes(b2_ref[...]) * INV_TURN - 0.25

    lhs_rows = PARTS * OWN
    pick = iota((lhs_rows, CHANS), 1) == own_first + DEVS * (iota((lhs_rows, CHANS), 0) & (OWN - 1))
    chosen = jnp.where(pick, 1.0, 0.0).astype(BF16)
    keep = iota((lhs_rows, wide), 1) >> 6 == iota((lhs_rows, wide), 0) >> 3
    hi_part = jnp.concatenate([hi_ref[...]] * PARTS, axis=0)
    fix_part = jnp.concatenate([(fix_ref[...].astype(F32) * 2.0 ** (-11)).astype(BF16)] * PARTS, axis=0)
    third_ref[...] = jnp.concatenate(
        [jnp.where(keep, dot_nt(chosen, hi_part), 0.0), jnp.where(keep, dot_nt(chosen, fix_part), 0.0)], axis=0
    ).astype(BF16)
    env_ref[...] = jnp.broadcast_to(
        jnp.sum(jnp.where(pick, decay_ref[...], 0.0), axis=1, keepdims=True), (lhs_rows, 128)
    )


def filter_step(step, first_ref, second_ref, bias_ref, third_ref, env_ref, filt_ref):
    lane = iota((1, 128), 1)
    where_in = (iota((STEP, 128), 0) + step * STEP).astype(F32)
    rate = ((lane & 15) + 1).astype(F32) * (1.0 / SEQ_LEN)
    shift = jnp.where((lane & 16) == 0, 0.0, 0.25)
    slope = jnp.where(lane < 100, 1.0 / QUARTER, 0.0)
    start = jnp.where((lane >= 100) & (lane < 103), 1.0, 0.0)
    turn = jnp.where((lane >= 103) & (lane < 106), float(TOP - QUARTER * (PARTS - 1)), float(SEQ_LEN))
    value = jnp.where(lane < 96, turn_cos(where_in * rate - shift), where_in * slope + start)
    value = jnp.where(where_in > turn, 1.0, value)
    low = ((lane >= 32) & (lane < 64)) | (lane == 97) | (lane == 99)
    high = value.astype(BF16).astype(F32)
    feats = jnp.where(low, value - high, high).astype(BF16)
    one_hi, one_lo = split_two(turn_cos(dot(feats, first_ref[...])))
    turns = dot(one_hi, second_ref[0]) + dot(one_lo, second_ref[0]) + dot(one_hi, second_ref[1])
    two_hi, two_lo = split_two(turn_cos(turns + bias_ref[...]))
    both = dot_nt(third_ref[...], two_hi) + dot_nt(third_ref[...], two_lo)
    lhs_rows = PARTS * OWN
    shape = (lhs_rows, STEP)
    time = TOP - QUARTER * ((iota(shape, 0) >> 3)) - (iota(shape, 1) + step * STEP)
    time = jnp.where(time < 0, time + SEQ_LEN, time).astype(F32)
    rate = jnp.concatenate([env_ref[...]] * (STEP // 128), axis=1)
    envelope = jnp.exp(-rate * time) * jnp.sqrt(2.0 * rate + 1.0 / SEQ_LEN)
    filters = (both[:lhs_rows] + both[lhs_rows:]) * envelope
    for tile in range(STEP // 128):
        filt_ref[step * (STEP // 128) + tile] = filters[:, 128 * tile:128 * (tile + 1)]


def toeplitz_tiles(filt_ref, toep_ref):
    shape = (TAP, 128)
    ahead = iota(shape, 1) >= iota(shape, 0)
    inside = iota(shape, 1) <= iota(shape, 0) + (128 - TAP)
    per_part = QUARTER // 128

    def slanted(part, tile):
        taps = filt_ref[tile, pl.ds(pl.multiple_of(part * OWN, OWN), OWN), :]
        return tuple(
            pltpu.roll(jnp.broadcast_to(taps[chan:chan + 1], shape), 0, 1, stride=1, stride_axis=0)
            for chan in range(OWN)
        )

    def block(index, before):
        part = lax.div(index, DEPTH_PER_PART)
        first = lax.rem(index, DEPTH_PER_PART) * (DEPTH // 128)
        for sub in range(DEPTH // 128):
            now = slanted(part, first + sub)
            for chan in range(OWN):
                tile = jnp.where(ahead, now[chan], before[chan])
                if sub == DEPTH // 128 - 1:
                    tile = jnp.where(inside | (index < SEQ_LEN // DEPTH - 1), tile, 0.0)
                toep_ref[chan, pl.ds(pl.multiple_of(index * TAP, TAP), TAP), sub * 128:(sub + 1) * 128] = tile.astype(BF16)
            before = now
        return before

    lax.fori_loop(0, SEQ_LEN // DEPTH, block, slanted(PARTS - 1, per_part - 1))


def signal_windows(chan, recv_ref, rows_ref, win_ref):
    lane = iota((128, 128), 1)
    before = recv_ref[pl.ds(SUB + chan, 128, stride=SUB), :]
    after = recv_ref[pl.ds(2 * SUB + chan, 128, stride=SUB), :]
    for sub in range(8):
        ahead = TAP * (sub + 1)
        value = after
        if ahead < 128:
            value = pltpu.roll(jnp.where(lane >= ahead, before, after), 128 - ahead, 1)
        rows_ref[pl.ds(56 + sub, 128, stride=8), :] = value
    win_ref[:, 0:128] = rows_ref[0:1072, :].astype(BF16)
    win_ref[:, 128:256] = rows_ref[8:1080, :].astype(BF16)


def convolve(chan, place, toep_ref, win_ref, conv_ref):
    sums = ([None] * 8, [None] * 8)
    for cols in range(4):
        window = jnp.concatenate(
            [win_ref[16 * deep + 256 * cols:16 * deep + 256 * (cols + 1), :] for deep in range(DEPTH // 256)], axis=1
        )
        part = dot_nt(toep_ref[chan, 64 * cols:256, :], window)
        for lag in range(16 - 4 * cols):
            row = TAP * (15 - lag - 4 * cols)
            for side in range(2):
                tile = 2 * cols + side + lag // 2
                if tile < 8:
                    piece = part[row:row + TAP, 128 * side:128 * (side + 1)]
                    old = sums[lag % 2][tile]
                    sums[lag % 2][tile] = piece if old is None else old + piece
    first_half = iota((TAP, 128), 1) < 64
    earlier = jnp.zeros((TAP, 128), F32)
    for tile in range(8):
        turned = pltpu.roll(sums[1][tile], 64, 1)
        conv_ref[tile, pl.ds(pl.multiple_of(place * TAP, TAP), TAP), :] = sums[0][tile] + jnp.where(
            first_half, earlier, turned
        )
        earlier = turned


def block_kernel(sig_ref, gate_ref, skip_ref, decay_ref, w1_ref, b1_ref, w2_ref, b2_ref, hi_ref, fix_ref, wout_ref,
                 out_ref,
                 first_ref, second_ref, bias_ref, third_ref, env_ref, filt_ref, toep_ref, rows_ref, win_ref, conv_ref,
                 send_x, recv_x, turn_ref, send_y0, send_y1, send_y2, recv_y0, recv_y1, recv_y2, gated_ref, wide_ref, total_ref, mixed_ref,
                 core_send, core_recv, far_send, far_recv,
                 wide_sem, x_send_sem, x_recv_sem, y_send_sem, y_recv_sem,
                 core_send_sem, core_recv_sem, far_send_sem, far_recv_sem, out_sem):
    me = lax.axis_index("seq")
    group = lax.axis_index("ch")
    core = lax.rem(group, 2)
    chip = lax.div(group, 2)
    core_mate = chip * 2 + 1 - core
    far_mate = (1 - chip) * 2 + core

    barrier = pltpu.get_barrier_semaphore()

    @pl.loop(1, DEVS)
    def _(step):
        pl.semaphore_signal(barrier, inc=1, device_id={"seq": lax.rem(me + step, DEVS)}, device_id_type=MESH)

    for mate in (core_mate, far_mate):
        pl.semaphore_signal(barrier, inc=1, device_id={"ch": mate}, device_id_type=MESH)

    blocks = ((1 - chip) * 2 + 1 - core, far_mate, core_mate, group)
    loads = [
        pltpu.make_async_copy(
            wout_ref.at[:, pl.ds(pl.multiple_of(block * COLS, COLS), COLS)], wide_ref.at[slot], wide_sem.at[slot]
        )
        for slot, block in enumerate(blocks)
    ]
    for load in loads:
        load.start()

    for half in range(2):
        turned = sig_ref[128 * half:128 * (half + 1), :].astype(F32).T
        for chan in range(OWN):
            send_x[chan // SUB, pl.ds(SUB * half + chan % SUB, DEVS, stride=8), :] = (
                turned[DEVS * chan:DEVS * (chan + 1), :]
            )
    own_send = pl.ds(pl.multiple_of(me * 8, 8), 8)
    own_recv = pl.ds(pl.multiple_of(me * 8 + 8, 8), 8)
    for group_num in range(2):
        recv_x[group_num, 0:8, :] = jnp.zeros((8, 128), F32)
        recv_x[group_num, own_recv, :] = send_x[group_num, own_send, :]
    filter_weights(me, decay_ref, w1_ref, b1_ref, w2_ref, b2_ref, hi_ref, fix_ref,
                   first_ref, second_ref, bias_ref, third_ref, env_ref)
    @pl.loop(0, 2)
    def _(step):
        filter_step(step, first_ref, second_ref, bias_ref, third_ref, env_ref, filt_ref)

    pl.semaphore_wait(barrier, DEVS + 1)

    for group_num in range(2):

        @pl.loop(1, DEVS)
        def _(step):
            peer = lax.rem(me + step, DEVS)
            pltpu.make_async_remote_copy(
                src_ref=send_x.at[group_num, pl.ds(pl.multiple_of(peer * 8, 8), 8), :],
                dst_ref=recv_x.at[group_num, own_recv, :],
                send_sem=x_send_sem.at[group_num],
                recv_sem=x_recv_sem.at[group_num],
                device_id={"seq": peer},
                device_id_type=MESH,
            ).start()

    @pl.loop(2, QUARTER // STEP)
    def _(step):
        filter_step(step, first_ref, second_ref, bias_ref, third_ref, env_ref, filt_ref)

    toeplitz_tiles(filt_ref, toep_ref)

    rows_ref[0:56, :] = jnp.zeros((56, 128), F32)
    pieces = ((0, 0, 8), (1, 0, 2), (1, 2, 6))
    outgoing, incoming = (send_y0, send_y1, send_y2), (recv_y0, recv_y1, recv_y2)

    def own_piece(size):
        return pl.ds(pl.multiple_of(me * size, 2), size)

    def return_rows(group_num):
        even_half = iota((64, 128), 1) < 64
        for tile in range(8):
            value = conv_ref[group_num, tile]
            turn_ref[tile] = jnp.concatenate([value, value], axis=0).T
            block = jnp.where(
                even_half, turn_ref[tile, pl.ds(0, 64, stride=2), :], turn_ref[tile, pl.ds(1, 64, stride=2), :]
            )
            for slot, (which, first, size) in enumerate(pieces):
                if which == group_num:
                    if size == 8:
                        outgoing[slot][64 * tile:64 * (tile + 1), :] = block
                    else:
                        for peer in range(8):
                            place = (8 * tile + peer) * size
                            row = 8 * peer + first
                            outgoing[slot][place:place + size, :] = block[row:row + size, :]
        for slot, (which, _, size) in enumerate(pieces):
            if which == group_num:
                incoming[slot][own_piece(size), :] = outgoing[slot][own_piece(size), :]

                @pl.loop(1, DEVS)
                def _(step):
                    peer = lax.rem(me + step, DEVS)
                    pltpu.make_async_remote_copy(
                        src_ref=outgoing[slot].at[pl.ds(pl.multiple_of(peer * size, 2), size), :],
                        dst_ref=incoming[slot].at[own_piece(size), :],
                        send_sem=y_send_sem.at[slot],
                        recv_sem=y_recv_sem.at[slot],
                        device_id={"seq": peer},
                        device_id_type=MESH,
                    ).start()

    def all_pieces(buffers, slot, sems):
        rows = pl.ds(0, (DEVS - 1) * pieces[slot][2])
        return pltpu.make_async_copy(buffers[slot].at[rows, :], buffers[slot].at[rows, :], sems.at[slot])

    many = pl.ds(0, (DEVS - 1) * 8)
    for group_num in range(2):
        pltpu.make_async_copy(
            recv_x.at[group_num, many, :], recv_x.at[group_num, many, :], x_recv_sem.at[group_num]
        ).wait()

        @pl.loop(0, SUB, unroll=2)
        def _(chan):
            signal_windows(chan, recv_x.at[group_num], rows_ref, win_ref)
            convolve(group_num * SUB + chan, chan, toep_ref, win_ref, conv_ref.at[group_num])

        return_rows(group_num)

    def to_core(quarter, which):
        return pltpu.make_async_remote_copy(
            src_ref=core_send.at[quarter, which], dst_ref=core_recv.at[quarter, which],
            send_sem=core_send_sem.at[quarter, which], recv_sem=core_recv_sem.at[quarter, which],
            device_id={"ch": core_mate}, device_id_type=MESH,
        )

    def to_far(quarter):
        return pltpu.make_async_remote_copy(
            src_ref=far_send.at[quarter], dst_ref=far_recv.at[quarter],
            send_sem=far_send_sem.at[quarter], recv_sem=far_recv_sem.at[quarter],
            device_id={"ch": far_mate}, device_id_type=MESH,
        )

    def to_out(quarter):
        return pltpu.make_async_copy(
            mixed_ref.at[quarter], out_ref.at[64 * quarter:64 * (quarter + 1), :], out_sem.at[quarter]
        )

    for load in loads:
        load.wait()
    first_half = iota((16, 128), 1) < 64
    for quarter in range(4):
        if quarter == 0:
            all_pieces(incoming, 0, y_recv_sem).wait()
        if quarter < 2:
            all_pieces(incoming, quarter + 1, y_recv_sem).wait()
        for row in range(2):
            if quarter == 0:
                late = recv_y1[pl.ds(row, DEVS, stride=2), :]
            else:
                late = recv_y2[pl.ds(2 * (quarter - 1) + row, DEVS, stride=6), :]
            both = jnp.concatenate([recv_y0[pl.ds(2 * quarter + row, DEVS, stride=8), :], late], axis=0).T
            swapped = pltpu.roll(both, 64, 1)
            for odd in range(2):
                place = 16 * (2 * row + odd)
                rows = slice(64 * quarter + place, 64 * quarter + place + 16)
                for two in range(OWN // 2):
                    left = 64 * odd + 32 * (two % 2)
                    low, high = slice(left, left + 16), slice(left + 16, left + 32)
                    lanes = slice(128 * two, 128 * (two + 1))
                    if two < 2:
                        value = jnp.where(first_half, both[low], swapped[high])
                    else:
                        value = jnp.where(first_half, swapped[low], both[high])
                    gated_ref[place:place + 16, lanes] = (
                        gate_ref[rows, lanes].astype(F32)
                        * (value + skip_ref[:, lanes] * sig_ref[rows, lanes].astype(F32))
                    ).astype(BF16)
        core_send[quarter, 0] = dot(gated_ref[...], wide_ref[0])
        to_core(quarter, 0).start()
        far_send[quarter] = dot(gated_ref[...], wide_ref[1])
        to_core(quarter, 0).wait_recv()
        far_send[quarter] += core_recv[quarter, 0]
        to_far(quarter).start()
        core_send[quarter, 1] = dot(gated_ref[...], wide_ref[2])
        to_core(quarter, 1).start()
        total_ref[quarter] = dot(gated_ref[...], wide_ref[3])
    for quarter in range(4):
        to_core(quarter, 1).wait_recv()
        to_far(quarter).wait_recv()
        mixed_ref[quarter] = (total_ref[quarter] + core_recv[quarter, 1] + far_recv[quarter]).astype(BF16)
        to_out(quarter).start()
    for quarter in range(4):
        to_out(quarter).wait()

    for group_num in range(2):
        pltpu.make_async_copy(
            send_x.at[group_num, many, :], send_x.at[group_num, many, :], x_send_sem.at[group_num]
        ).wait()
    for slot in range(3):
        all_pieces(outgoing, slot, y_send_sem).wait()
    for quarter in range(4):
        for which in range(2):
            to_core(quarter, which).wait_send()
        to_far(quarter).wait_send()


def shards(signal, gate_in, skip_gain, decay, pos_weight1, pos_bias1, pos_weight2, pos_bias2, filt_hi, filt_fix,
           out_weight):
    vmem = pl.BlockSpec(memory_space=pltpu.VMEM)
    wide = PARTS * HID
    return pl.pallas_call(
        block_kernel,
        out_shape=jax.ShapeDtypeStruct((ROWS, COLS), BF16),
        in_specs=[vmem] * 10 + [pl.BlockSpec(memory_space=pl.ANY)],
        out_specs=pl.BlockSpec(memory_space=pl.ANY),
        scratch_shapes=[
            pltpu.VMEM((128, wide), BF16),
            pltpu.VMEM((2, wide, wide), BF16),
            pltpu.VMEM((1, wide), F32),
            pltpu.VMEM((2 * PARTS * OWN, wide), BF16),
            pltpu.VMEM((PARTS * OWN, 128), F32),
            pltpu.VMEM((QUARTER // 128, PARTS * OWN, 128), F32),
            pltpu.VMEM((OWN, SEQ_LEN // DEPTH * TAP, DEPTH), BF16),
            pltpu.VMEM((1088, 128), F32),
            pltpu.VMEM((1072, 256), BF16),
            pltpu.VMEM((2, 8, SUB * TAP, 128), F32),
            pltpu.VMEM((2, DEVS * 8, 128), F32),
            pltpu.VMEM((2, DEVS * 8 + 8, 128), F32),
            pltpu.VMEM((8, 128, 128), F32),
            pltpu.VMEM((DEVS * 8, 128), F32),
            pltpu.VMEM((DEVS * 2, 128), F32),
            pltpu.VMEM((DEVS * 6, 128), F32),
            pltpu.VMEM((DEVS * 8, 128), F32),
            pltpu.VMEM((DEVS * 2, 128), F32),
            pltpu.VMEM((DEVS * 6, 128), F32),
            pltpu.VMEM((64, CHANS), BF16),
            pltpu.VMEM((4, CHANS, COLS), BF16),
            pltpu.VMEM((4, 64, COLS), F32),
            pltpu.VMEM((4, 64, COLS), BF16),
            pltpu.VMEM((4, 2, 64, COLS), F32),
            pltpu.VMEM((4, 2, 64, COLS), F32),
            pltpu.VMEM((4, 64, COLS), F32),
            pltpu.VMEM((4, 64, COLS), F32),
            pltpu.SemaphoreType.DMA((4,)),
            pltpu.SemaphoreType.DMA((2,)),
            pltpu.SemaphoreType.DMA((2,)),
            pltpu.SemaphoreType.DMA((4,)),
            pltpu.SemaphoreType.DMA((4,)),
            pltpu.SemaphoreType.DMA((4, 2)),
            pltpu.SemaphoreType.DMA((4, 2)),
            pltpu.SemaphoreType.DMA((4,)),
            pltpu.SemaphoreType.DMA((4,)),
            pltpu.SemaphoreType.DMA((4,)),
        ],
        compiler_params=pltpu.CompilerParams(
            collective_id=0, has_side_effects=True, vmem_limit_bytes=56 * 2**20
        ),
        name="hyena_block",
    )(
        signal, gate_in, skip_gain[None, :], decay[None, :], pos_weight1, pos_bias1[None, :], pos_weight2,
        pos_bias2[None, :], filt_hi, filt_fix, out_weight,
    )


def solution(mesh):
    return jax.shard_map(
        shards,
        mesh=mesh,
        in_specs=(
            P("seq", "ch"), P("seq", "ch"), P("ch"), P("ch"), P(), P(), P(), P(), P(None, "ch"), P(None, "ch"),
            P("ch", None),
        ),
        out_specs=P("seq", "ch"),
        check_vma=False,
    )
```

```python
import math

import jax
import jax.numpy as jnp
from jax import lax
from jax.experimental import pallas as pl
from jax.experimental.pallas import tpu as pltpu
from jax.sharding import PartitionSpec as P

F32 = jnp.float32
BF16 = jnp.bfloat16
MESH = pl.DeviceIdType.MESH

SEQ_LEN = 16384
DEVS = 64
ROWS = 256
CHANS = 512
OWN = 8
SUB = 4
HID = 64
PARTS = 4
QUARTER = SEQ_LEN // PARTS
STEP = 1024
TAP = 16
DEPTH = 1024
DEPTH_PER_PART = QUARTER // DEPTH
TOP = SEQ_LEN - TAP
COLS = 1024
INV_TURN = 1.0 / (2.0 * math.pi)
COS_POLY = (6.283185159611168, -41.34165492934356, 81.60099819261757, -76.54965682073457, 39.53581371237487)


def turn_cos(turns):
    near = turns - jnp.round(turns)
    arg = 0.25 - jnp.abs(near)
    square = arg * arg
    c0, c1, c2, c3, c4 = COS_POLY
    return arg * (c0 + square * (c1 + square * (c2 + square * (c3 + square * c4))))


def split_two(value):
    high = value.astype(BF16)
    return high, (value - high.astype(F32)).astype(BF16)


def dot(left, right):
    return jnp.dot(left, right, preferred_element_type=F32)


def dot_nt(left, right):
    return lax.dot_general(left, right, (((1,), (1,)), ((), ())), preferred_element_type=F32)


def tile_lanes(value):
    return jnp.concatenate([value] * PARTS, axis=1)


def iota(shape, axis):
    return lax.broadcasted_iota(jnp.int32, shape, axis)


def filter_weights(own_first, decay_ref, w1_ref, b1_ref, w2_ref, b2_ref, hi_ref, fix_ref,
                   first_ref, second_ref, bias_ref, third_ref, env_ref):
    wide = PARTS * HID
    part = iota((16, wide), 1) >> 6
    freq = (iota((16, wide), 0) + 1).astype(F32)
    turns = freq * (TOP - QUARTER * part).astype(F32) * (1.0 / SEQ_LEN)
    cos_top, sin_top = turn_cos(turns), turn_cos(turns - 0.25)
    w_lin = tile_lanes(w1_ref[0:1, :]) * INV_TURN
    w_cos = tile_lanes(w1_ref[1:17, :]) * INV_TURN
    w_sin = tile_lanes(w1_ref[17:33, :]) * INV_TURN
    main = jnp.concatenate(
        [w_cos * cos_top + w_sin * sin_top, w_cos * sin_top - w_sin * cos_top], axis=0
    )
    main_hi = main.astype(BF16).astype(F32)
    main_lo = main - main_hi
    part_row = iota((1, wide), 1) >> 6
    top_row = (TOP - QUARTER * part_row).astype(F32) * (1.0 / SEQ_LEN)
    slope = -w_lin / PARTS
    const = w_lin * top_row + tile_lanes(b1_ref[...]) * INV_TURN - 0.25
    wrap = jnp.where(part_row == PARTS - 1, w_lin, 0.0)
    extra = jnp.zeros((32, wide), F32)
    row = iota((32, wide), 0)
    place = 0
    for value, pieces, repeat in ((slope, 2, 2), (const, 3, 1), (wrap, 3, 1)):
        rest = value
        for _ in range(pieces):
            piece = rest.astype(BF16).astype(F32)
            rest = rest - piece
            for _ in range(repeat):
                extra = jnp.where(row == place, piece, extra)
                place += 1
    first_ref[...] = jnp.concatenate([main_hi, main_hi, main_lo, extra], axis=0).astype(BF16)

    own_block = iota((wide, wide), 0) >> 6 == iota((wide, wide), 1) >> 6
    w2_rows = jnp.concatenate([w2_ref[...] * INV_TURN] * PARTS, axis=0)
    w2_full = jnp.where(own_block, tile_lanes(w2_rows), 0.0)
    w2_hi, w2_lo = split_two(w2_full)
    second_ref[0] = w2_hi
    second_ref[1] = w2_lo
    bias_ref[...] = tile_lanes(b2_ref[...]) * INV_TURN - 0.25

    lhs_rows = PARTS * OWN
    pick = iota((lhs_rows, CHANS), 1) == own_first + DEVS * (iota((lhs_rows, CHANS), 0) & (OWN - 1))
    chosen = jnp.where(pick, 1.0, 0.0).astype(BF16)
    keep = iota((lhs_rows, wide), 1) >> 6 == iota((lhs_rows, wide), 0) >> 3
    hi_part = jnp.concatenate([hi_ref[...]] * PARTS, axis=0)
    fix_part = jnp.concatenate([(fix_ref[...].astype(F32) * 2.0 ** (-11)).astype(BF16)] * PARTS, axis=0)
    third_ref[...] = jnp.concatenate(
        [jnp.where(keep, dot_nt(chosen, hi_part), 0.0), jnp.where(keep, dot_nt(chosen, fix_part), 0.0)], axis=0
    ).astype(BF16)
    env_ref[...] = jnp.broadcast_to(
        jnp.sum(jnp.where(pick, decay_ref[...], 0.0), axis=1, keepdims=True), (lhs_rows, 128)
    )


def filter_step(step, first_ref, second_ref, bias_ref, third_ref, env_ref, filt_ref):
    lane = iota((1, 128), 1)
    where_in = (iota((STEP, 128), 0) + step * STEP).astype(F32)
    rate = ((lane & 15) + 1).astype(F32) * (1.0 / SEQ_LEN)
    shift = jnp.where((lane & 16) == 0, 0.0, 0.25)
    slope = jnp.where(lane < 100, 1.0 / QUARTER, 0.0)
    start = jnp.where((lane >= 100) & (lane < 103), 1.0, 0.0)
    turn = jnp.where((lane >= 103) & (lane < 106), float(TOP - QUARTER * (PARTS - 1)), float(SEQ_LEN))
    value = jnp.where(lane < 96, turn_cos(where_in * rate - shift), where_in * slope + start)
    value = jnp.where(where_in > turn, 1.0, value)
    low = ((lane >= 32) & (lane < 64)) | (lane == 97) | (lane == 99)
    high = value.astype(BF16).astype(F32)
    feats = jnp.where(low, value - high, high).astype(BF16)
    one_hi, one_lo = split_two(turn_cos(dot(feats, first_ref[...])))
    turns = dot(one_hi, second_ref[0]) + dot(one_lo, second_ref[0]) + dot(one_hi, second_ref[1])
    two_hi, two_lo = split_two(turn_cos(turns + bias_ref[...]))
    both = dot_nt(third_ref[...], two_hi) + dot_nt(third_ref[...], two_lo)
    lhs_rows = PARTS * OWN
    shape = (lhs_rows, STEP)
    time = TOP - QUARTER * ((iota(shape, 0) >> 3)) - (iota(shape, 1) + step * STEP)
    time = jnp.where(time < 0, time + SEQ_LEN, time).astype(F32)
    rate = jnp.concatenate([env_ref[...]] * (STEP // 128), axis=1)
    envelope = jnp.exp(-rate * time) * jnp.sqrt(2.0 * rate + 1.0 / SEQ_LEN)
    filters = (both[:lhs_rows] + both[lhs_rows:]) * envelope
    for tile in range(STEP // 128):
        filt_ref[step * (STEP // 128) + tile] = filters[:, 128 * tile:128 * (tile + 1)]


def toeplitz_tiles(filt_ref, toep_ref):
    shape = (TAP, 128)
    ahead = iota(shape, 1) >= iota(shape, 0)
    inside = iota(shape, 1) <= iota(shape, 0) + (128 - TAP)
    per_part = QUARTER // 128

    def slanted(part, tile):
        taps = filt_ref[tile, pl.ds(pl.multiple_of(part * OWN, OWN), OWN), :]
        return tuple(
            pltpu.roll(jnp.broadcast_to(taps[chan:chan + 1], shape), 0, 1, stride=1, stride_axis=0)
            for chan in range(OWN)
        )

    def block(index, before):
        part = lax.div(index, DEPTH_PER_PART)
        first = lax.rem(index, DEPTH_PER_PART) * (DEPTH // 128)
        for sub in range(DEPTH // 128):
            now = slanted(part, first + sub)
            for chan in range(OWN):
                tile = jnp.where(ahead, now[chan], before[chan])
                if sub == DEPTH // 128 - 1:
                    tile = jnp.where(inside | (index < SEQ_LEN // DEPTH - 1), tile, 0.0)
                toep_ref[chan, pl.ds(pl.multiple_of(index * TAP, TAP), TAP), sub * 128:(sub + 1) * 128] = tile.astype(BF16)
            before = now
        return before

    lax.fori_loop(0, SEQ_LEN // DEPTH, block, slanted(PARTS - 1, per_part - 1))


def signal_windows(chan, recv_ref, rows_ref, win_ref):
    lane = iota((128, 128), 1)
    before = recv_ref[pl.ds(SUB + chan, 128, stride=SUB), :]
    after = recv_ref[pl.ds(2 * SUB + chan, 128, stride=SUB), :]
    for sub in range(8):
        ahead = TAP * (sub + 1)
        value = after
        if ahead < 128:
            value = pltpu.roll(jnp.where(lane >= ahead, before, after), 128 - ahead, 1)
        rows_ref[pl.ds(56 + sub, 128, stride=8), :] = value
    win_ref[:, 0:128] = rows_ref[0:1072, :].astype(BF16)
    win_ref[:, 128:256] = rows_ref[8:1080, :].astype(BF16)


def convolve(chan, place, toep_ref, win_ref, conv_ref):
    sums = ([None] * 8, [None] * 8)
    for cols in range(4):
        window = jnp.concatenate(
            [win_ref[16 * deep + 256 * cols:16 * deep + 256 * (cols + 1), :] for deep in range(DEPTH // 256)], axis=1
        )
        part = dot_nt(toep_ref[chan, 64 * cols:256, :], window)
        for lag in range(16 - 4 * cols):
            row = TAP * (15 - lag - 4 * cols)
            for side in range(2):
                tile = 2 * cols + side + lag // 2
                if tile < 8:
                    piece = part[row:row + TAP, 128 * side:128 * (side + 1)]
                    old = sums[lag % 2][tile]
                    sums[lag % 2][tile] = piece if old is None else old + piece
    first_half = iota((TAP, 128), 1) < 64
    earlier = jnp.zeros((TAP, 128), F32)
    for tile in range(8):
        turned = pltpu.roll(sums[1][tile], 64, 1)
        conv_ref[tile, pl.ds(pl.multiple_of(place * TAP, TAP), TAP), :] = sums[0][tile] + jnp.where(
            first_half, earlier, turned
        )
        earlier = turned


def block_kernel(sig_ref, gate_ref, skip_ref, decay_ref, w1_ref, b1_ref, w2_ref, b2_ref, hi_ref, fix_ref, wout_ref,
                 out_ref,
                 first_ref, second_ref, bias_ref, third_ref, env_ref, filt_ref, toep_ref, rows_ref, win_ref, conv_ref,
                 send_x, recv_x, turn_ref, send_y0, send_y1, send_y2, recv_y0, recv_y1, recv_y2, gated_ref, wide_ref, total_ref, mixed_ref,
                 core_send, core_recv, far_send, far_recv,
                 wide_sem, x_send_sem, x_recv_sem, y_send_sem, y_recv_sem,
                 core_send_sem, core_recv_sem, far_send_sem, far_recv_sem, out_sem):
    me = lax.axis_index("seq")
    group = lax.axis_index("ch")
    core = lax.rem(group, 2)
    chip = lax.div(group, 2)
    core_mate = chip * 2 + 1 - core
    far_mate = (1 - chip) * 2 + core

    barrier = pltpu.get_barrier_semaphore()

    @pl.loop(1, DEVS)
    def _(step):
        pl.semaphore_signal(barrier, inc=1, device_id={"seq": lax.rem(me + step, DEVS)}, device_id_type=MESH)

    for mate in (core_mate, far_mate):
        pl.semaphore_signal(barrier, inc=1, device_id={"ch": mate}, device_id_type=MESH)

    blocks = ((1 - chip) * 2 + 1 - core, far_mate, core_mate, group)
    loads = [
        pltpu.make_async_copy(
            wout_ref.at[:, pl.ds(pl.multiple_of(block * COLS, COLS), COLS)], wide_ref.at[slot], wide_sem.at[slot]
        )
        for slot, block in enumerate(blocks)
    ]
    for load in loads:
        load.start()

    for half in range(2):
        turned = sig_ref[128 * half:128 * (half + 1), :].astype(F32).T
        for chan in range(OWN):
            send_x[chan // SUB, pl.ds(SUB * half + chan % SUB, DEVS, stride=8), :] = (
                turned[DEVS * chan:DEVS * (chan + 1), :]
            )
    own_send = pl.ds(pl.multiple_of(me * 8, 8), 8)
    own_recv = pl.ds(pl.multiple_of(me * 8 + 8, 8), 8)
    for group_num in range(2):
        recv_x[group_num, 0:8, :] = jnp.zeros((8, 128), F32)
        recv_x[group_num, own_recv, :] = send_x[group_num, own_send, :]
    filter_weights(me, decay_ref, w1_ref, b1_ref, w2_ref, b2_ref, hi_ref, fix_ref,
                   first_ref, second_ref, bias_ref, third_ref, env_ref)
    @pl.loop(0, 2)
    def _(step):
        filter_step(step, first_ref, second_ref, bias_ref, third_ref, env_ref, filt_ref)

    pl.semaphore_wait(barrier, DEVS + 1)

    for group_num in range(2):

        @pl.loop(1, DEVS)
        def _(step):
            peer = lax.rem(me + step, DEVS)
            pltpu.make_async_remote_copy(
                src_ref=send_x.at[group_num, pl.ds(pl.multiple_of(peer * 8, 8), 8), :],
                dst_ref=recv_x.at[group_num, own_recv, :],
                send_sem=x_send_sem.at[group_num],
                recv_sem=x_recv_sem.at[group_num],
                device_id={"seq": peer},
                device_id_type=MESH,
            ).start()

    @pl.loop(2, QUARTER // STEP)
    def _(step):
        filter_step(step, first_ref, second_ref, bias_ref, third_ref, env_ref, filt_ref)

    toeplitz_tiles(filt_ref, toep_ref)

    rows_ref[0:56, :] = jnp.zeros((56, 128), F32)
    pieces = ((0, 0, 8), (1, 0, 2), (1, 2, 6))
    outgoing, incoming = (send_y0, send_y1, send_y2), (recv_y0, recv_y1, recv_y2)

    def own_piece(size):
        return pl.ds(pl.multiple_of(me * size, 2), size)

    def return_rows(group_num):
        even_half = iota((64, 128), 1) < 64
        for slot, (which, first, size) in enumerate(pieces):
            if which == group_num:
                for tile in range(8):
                    if first == 0:
                        value = conv_ref[group_num, tile]
                        turn_ref[tile] = jnp.concatenate([value, value], axis=0).T
                    block = jnp.where(
                        even_half, turn_ref[tile, pl.ds(0, 64, stride=2), :], turn_ref[tile, pl.ds(1, 64, stride=2), :]
                    )
                    if size == 8:
                        outgoing[slot][64 * tile:64 * (tile + 1), :] = block
                    else:
                        for peer in range(8):
                            place = (8 * tile + peer) * size
                            row = 8 * peer + first
                            outgoing[slot][place:place + size, :] = block[row:row + size, :]
                incoming[slot][own_piece(size), :] = outgoing[slot][own_piece(size), :]

                @pl.loop(1, DEVS)
                def _(step):
                    peer = lax.rem(me + step, DEVS)
                    pltpu.make_async_remote_copy(
                        src_ref=outgoing[slot].at[pl.ds(pl.multiple_of(peer * size, 2), size), :],
                        dst_ref=incoming[slot].at[own_piece(size), :],
                        send_sem=y_send_sem.at[slot],
                        recv_sem=y_recv_sem.at[slot],
                        device_id={"seq": peer},
                        device_id_type=MESH,
                    ).start()

    def all_pieces(buffers, slot, sems):
        rows = pl.ds(0, (DEVS - 1) * pieces[slot][2])
        return pltpu.make_async_copy(buffers[slot].at[rows, :], buffers[slot].at[rows, :], sems.at[slot])

    many = pl.ds(0, (DEVS - 1) * 8)
    for group_num in range(2):
        pltpu.make_async_copy(
            recv_x.at[group_num, many, :], recv_x.at[group_num, many, :], x_recv_sem.at[group_num]
        ).wait()

        @pl.loop(0, SUB, unroll=4)
        def _(chan):
            signal_windows(chan, recv_x.at[group_num], rows_ref, win_ref)
            convolve(group_num * SUB + chan, chan, toep_ref, win_ref, conv_ref.at[group_num])

        return_rows(group_num)

    def to_core(quarter, which):
        return pltpu.make_async_remote_copy(
            src_ref=core_send.at[quarter, which], dst_ref=core_recv.at[quarter, which],
            send_sem=core_send_sem.at[quarter, which], recv_sem=core_recv_sem.at[quarter, which],
            device_id={"ch": core_mate}, device_id_type=MESH,
        )

    def to_far(quarter):
        return pltpu.make_async_remote_copy(
            src_ref=far_send.at[quarter], dst_ref=far_recv.at[quarter],
            send_sem=far_send_sem.at[quarter], recv_sem=far_recv_sem.at[quarter],
            device_id={"ch": far_mate}, device_id_type=MESH,
        )

    def to_out(quarter):
        return pltpu.make_async_copy(
            mixed_ref.at[quarter], out_ref.at[64 * quarter:64 * (quarter + 1), :], out_sem.at[quarter]
        )

    for load in loads:
        load.wait()
    first_half = iota((16, 128), 1) < 64
    for quarter in range(4):
        if quarter == 0:
            all_pieces(incoming, 0, y_recv_sem).wait()
        if quarter < 2:
            all_pieces(incoming, quarter + 1, y_recv_sem).wait()
        for row in range(2):
            if quarter == 0:
                late = recv_y1[pl.ds(row, DEVS, stride=2), :]
            else:
                late = recv_y2[pl.ds(2 * (quarter - 1) + row, DEVS, stride=6), :]
            both = jnp.concatenate([recv_y0[pl.ds(2 * quarter + row, DEVS, stride=8), :], late], axis=0).T
            swapped = pltpu.roll(both, 64, 1)
            for odd in range(2):
                place = 16 * (2 * row + odd)
                rows = slice(64 * quarter + place, 64 * quarter + place + 16)
                for two in range(OWN // 2):
                    left = 64 * odd + 32 * (two % 2)
                    low, high = slice(left, left + 16), slice(left + 16, left + 32)
                    lanes = slice(128 * two, 128 * (two + 1))
                    if two < 2:
                        value = jnp.where(first_half, both[low], swapped[high])
                    else:
                        value = jnp.where(first_half, swapped[low], both[high])
                    gated_ref[place:place + 16, lanes] = (
                        gate_ref[rows, lanes].astype(F32)
                        * (value + skip_ref[:, lanes] * sig_ref[rows, lanes].astype(F32))
                    ).astype(BF16)
        core_send[quarter, 0] = dot(gated_ref[...], wide_ref[0])
        to_core(quarter, 0).start()
        far_send[quarter] = dot(gated_ref[...], wide_ref[1])
        to_core(quarter, 0).wait_recv()
        far_send[quarter] += core_recv[quarter, 0]
        to_far(quarter).start()
        core_send[quarter, 1] = dot(gated_ref[...], wide_ref[2])
        to_core(quarter, 1).start()
        total_ref[quarter] = dot(gated_ref[...], wide_ref[3])
    for quarter in range(4):
        to_core(quarter, 1).wait_recv()
        to_far(quarter).wait_recv()
        mixed_ref[quarter] = (total_ref[quarter] + core_recv[quarter, 1] + far_recv[quarter]).astype(BF16)
        to_out(quarter).start()
    for quarter in range(4):
        to_out(quarter).wait()

    for group_num in range(2):
        pltpu.make_async_copy(
            send_x.at[group_num, many, :], send_x.at[group_num, many, :], x_send_sem.at[group_num]
        ).wait()
    for slot in range(3):
        all_pieces(outgoing, slot, y_send_sem).wait()
    for quarter in range(4):
        for which in range(2):
            to_core(quarter, which).wait_send()
        to_far(quarter).wait_send()


def shards(signal, gate_in, skip_gain, decay, pos_weight1, pos_bias1, pos_weight2, pos_bias2, filt_hi, filt_fix,
           out_weight):
    vmem = pl.BlockSpec(memory_space=pltpu.VMEM)
    wide = PARTS * HID
    return pl.pallas_call(
        block_kernel,
        out_shape=jax.ShapeDtypeStruct((ROWS, COLS), BF16),
        in_specs=[vmem] * 10 + [pl.BlockSpec(memory_space=pl.ANY)],
        out_specs=pl.BlockSpec(memory_space=pl.ANY),
        scratch_shapes=[
            pltpu.VMEM((128, wide), BF16),
            pltpu.VMEM((2, wide, wide), BF16),
            pltpu.VMEM((1, wide), F32),
            pltpu.VMEM((2 * PARTS * OWN, wide), BF16),
            pltpu.VMEM((PARTS * OWN, 128), F32),
            pltpu.VMEM((QUARTER // 128, PARTS * OWN, 128), F32),
            pltpu.VMEM((OWN, SEQ_LEN // DEPTH * TAP, DEPTH), BF16),
            pltpu.VMEM((1088, 128), F32),
            pltpu.VMEM((1072, 256), BF16),
            pltpu.VMEM((2, 8, SUB * TAP, 128), F32),
            pltpu.VMEM((2, DEVS * 8, 128), F32),
            pltpu.VMEM((2, DEVS * 8 + 8, 128), F32),
            pltpu.VMEM((8, 128, 128), F32),
            pltpu.VMEM((DEVS * 8, 128), F32),
            pltpu.VMEM((DEVS * 2, 128), F32),
            pltpu.VMEM((DEVS * 6, 128), F32),
            pltpu.VMEM((DEVS * 8, 128), F32),
            pltpu.VMEM((DEVS * 2, 128), F32),
            pltpu.VMEM((DEVS * 6, 128), F32),
            pltpu.VMEM((64, CHANS), BF16),
            pltpu.VMEM((4, CHANS, COLS), BF16),
            pltpu.VMEM((4, 64, COLS), F32),
            pltpu.VMEM((4, 64, COLS), BF16),
            pltpu.VMEM((4, 2, 64, COLS), F32),
            pltpu.VMEM((4, 2, 64, COLS), F32),
            pltpu.VMEM((4, 64, COLS), F32),
            pltpu.VMEM((4, 64, COLS), F32),
            pltpu.SemaphoreType.DMA((4,)),
            pltpu.SemaphoreType.DMA((2,)),
            pltpu.SemaphoreType.DMA((2,)),
            pltpu.SemaphoreType.DMA((4,)),
            pltpu.SemaphoreType.DMA((4,)),
            pltpu.SemaphoreType.DMA((4, 2)),
            pltpu.SemaphoreType.DMA((4, 2)),
            pltpu.SemaphoreType.DMA((4,)),
            pltpu.SemaphoreType.DMA((4,)),
            pltpu.SemaphoreType.DMA((4,)),
        ],
        compiler_params=pltpu.CompilerParams(
            collective_id=0, has_side_effects=True, vmem_limit_bytes=56 * 2**20
        ),
        name="hyena_block",
    )(
        signal, gate_in, skip_gain[None, :], decay[None, :], pos_weight1, pos_bias1[None, :], pos_weight2,
        pos_bias2[None, :], filt_hi, filt_fix, out_weight,
    )


def solution(mesh):
    return jax.shard_map(
        shards,
        mesh=mesh,
        in_specs=(
            P("seq", "ch"), P("seq", "ch"), P("ch"), P("ch"), P(), P(), P(), P(), P(None, "ch"), P(None, "ch"),
            P("ch", None),
        ),
        out_specs=P("seq", "ch"),
        check_vma=False,
    )
```
